32 devices in a mesh: rep: 2 (over y), ctx: 4 (over z), head: 2 (over x), sub: 2 (over core).
Axes of the slice: x: 2, y: 2, z: 4, core: 2. Of those that a mesh axis runs over, the one named last changes fastest.
Arguments:
- hidden_states: bfloat16 [2048, 4096], P(('rep', 'ctx'), ('head', 'sub')), parts along dimension 0, may hold values from -8 to 8
- w_query: bfloat16 [4096, 2048], P('ctx', ('head', 'sub')), may hold values from -0.09375 to 0.09375
- w_key: bfloat16 [4096, 2048], P('ctx', ('head', 'sub')), may hold values from -0.09375 to 0.09375
- w_value: bfloat16 [4096, 2048], P('ctx', ('head', 'sub')), may hold values from -0.09375 to 0.09375
- a_query: bfloat16 [4096, 8], replicated, may hold values from -0.09375 to 0.09375
- a_value: bfloat16 [4096, 8], replicated, may hold values from -0.09375 to 0.09375
- b_query: bfloat16 [8, 2048], P(None, ('head', 'sub')), may hold values from -0.29882812 to 0.29882812
- b_value: bfloat16 [8, 2048], P(None, ('head', 'sub')), may hold values from -0.29882812 to 0.29882812
- positions: int32 [2048], P(('rep', 'ctx')), parts along dimension 0, may hold values from 0 to 99999, as said below
- out_grad: bfloat16 [2048, 2048], P(('rep', 'ctx'), ('head', 'sub')), parts along dimension 0, may hold values from -0.119628906 to 0.119628906
Outputs:
- attn_out: bfloat16 [2048, 2048], P(('rep', 'ctx'), ('head', 'sub')), parts along dimension 0
- grad_a_query: float32 [4096, 16], P(None, 'rep'), parts along dimension 1
- grad_b_query: float32 [16, 2048], P('rep', ('head', 'sub')), parts along dimension 0
- grad_a_value: float32 [4096, 16], P(None, 'rep'), parts along dimension 1
- grad_b_value: float32 [16, 2048], P('rep', ('head', 'sub')), parts along dimension 0
The draws below stay inside these ranges and needn't reach their ends.
There are 2 independent parts, one for each index of `rep`. The reference program is written for one: setup_inputs(seed, part) draws one part's arguments, and reference() takes and returns one part's arrays. A program takes and returns all parts, laid end to end along the dimension named above; an argument that names none is the same for every part. Nothing has to cross between parts.
Inputs may be any that keep to these rules, and one draw needn't show every extreme that they name: `positions`: strictly increasing along the sequence; the first is 0 and the last is 99999.
All inputs are finite; a program needn't handle non-finite values.
Results may differ from the reference program's by a relative error of at most 0.012.
Values may be sent and summed in bfloat16 or wider, within the bound.
A program may use at most 64 MiB of HBM per device.

```python
import math
import jax
import jax.numpy as jnp
from jax import lax

D = 4096
HEAD_DIM = 128
HEADS = 16
RANK = 8
TRAIN_CTX = 4096
MAX_POS = 100000
HD = 2048
TOKENS = 1024
GROUP = 256


def draw_hidden_states(key, part):
    normal_key = jax.random.fold_in(jax.random.fold_in(key, 11), 0)
    entries = jnp.clip(jax.random.normal(normal_key, (TOKENS, D), jnp.float32), -4.0, 4.0)
    return entries.astype(jnp.bfloat16)


def draw_positions(key, part):
    cut_key, split_key = jax.random.split(jax.random.fold_in(key, 23))
    cuts = jnp.sort(jax.random.randint(cut_key, (3,), 1, TOKENS))
    extra = MAX_POS - TOKENS
    splits = jnp.sort(jax.random.randint(split_key, (2,), 0, extra + 1))
    jumps = jnp.stack([splits[0], splits[1] - splits[0], extra - splits[1]])
    steps_along = jnp.arange(TOKENS, dtype=jnp.int32)
    skipped = jnp.sum(jnp.where(steps_along[:, None] >= cuts[None, :], jumps[None, :], 0), axis=1)
    return (steps_along + skipped).astype(jnp.int32)


def levels(key, shape, shards, least, largest):
    loudness, own = 1.0, jax.random.fold_in(key, 6)
    for axis_at, shards_of in shards:
        draws = jnp.exp(jax.random.uniform(jax.random.fold_in(own, axis_at), (shards_of,), jnp.float32, least / len(shards), largest / len(shards)))
        loudness = loudness * jnp.repeat(draws, shape[axis_at] // shards_of).reshape([-1 if axis == axis_at else 1 for axis in range(len(shape))])
    return loudness


def gaussian(rng, extent, deviation, reach, shards=(), held_as=jnp.bfloat16):
    drawn = jax.random.normal(rng, extent, jnp.float32) * deviation
    if len(shards) > 0:
        drawn = levels(rng, extent, shards, -0.22, 0.18) * drawn
    return jnp.clip(drawn, min=-reach, max=reach).astype(held_as)


def setup_inputs(seed: int = 0, part: int = 0) -> dict:
    streams_of = jax.random.split(jax.random.key(seed), 11)
    part_keys = jax.random.split(jax.random.fold_in(streams_of[10], part), 11)
    hidden_states = draw_hidden_states(jax.random.fold_in(jax.random.fold_in(streams_of[10], part), 71), part)
    w_query = gaussian(streams_of[1], (D, HD), D ** -0.5, 0.09375, ((0, 4), (1, 4)))
    w_key = gaussian(streams_of[2], (D, HD), D ** -0.5, 0.09375, ((0, 4), (1, 4)))
    w_value = gaussian(streams_of[3], (D, HD), D ** -0.5, 0.09375, ((0, 4), (1, 4)))
    a_query = gaussian(streams_of[4], (D, RANK), D ** -0.5, 0.09375)
    a_value = gaussian(streams_of[5], (D, RANK), D ** -0.5, 0.09375)
    b_query = gaussian(streams_of[6], (RANK, HD), 0.05, 0.29882812, ((1, 4),))
    b_value = gaussian(streams_of[7], (RANK, HD), 0.05, 0.29882812, ((1, 4),))
    positions = draw_positions(jax.random.fold_in(jax.random.fold_in(streams_of[10], part), 71), part)
    out_grad = gaussian(part_keys[9], (TOKENS, HD), 0.02, 0.119628906, ((0, 4), (1, 4)))
    return {"hidden_states": hidden_states, "w_query": w_query, "w_key": w_key, "w_value": w_value, "a_query": a_query, "a_value": a_value, "b_query": b_query, "b_value": b_value, "positions": positions, "out_grad": out_grad}


def rope_tables(positions):
    half_dim = HEAD_DIM // 2
    inverse = jnp.exp(jnp.arange(half_dim, dtype=jnp.float32) * (-2.0 * math.log(10000.0) / HEAD_DIM))
    scaled = positions.astype(jnp.float32) * (TRAIN_CTX / MAX_POS)
    angle = scaled[:, None] * inverse[None, :]
    return (jnp.cos(angle)[:, None, :], jnp.sin(angle)[:, None, :])

def rotate(vectors, cosine, sine):
    half_dim = vectors.shape[-1] // 2
    first = vectors[..., :half_dim]
    second = vectors[..., half_dim:]
    return jnp.concatenate([first * cosine - second * sine, second * cosine + first * sine], axis=-1)

def head_pass(operands):
    queries, keys, values, grads, moved = operands
    amount = moved * (GROUP // 2)
    groups = TOKENS // GROUP
    scale = 1.0 / math.sqrt(HEAD_DIM)

    def arrange(tensor):
        return jnp.roll(tensor, -amount, axis=0).reshape(groups, GROUP, HEAD_DIM).astype(jnp.float32)
    query_f, key_f, value_f, grad_f = (arrange(queries), arrange(keys), arrange(values), arrange(grads))
    allowed = jnp.arange(GROUP)[:, None] >= jnp.arange(GROUP)[None, :]
    scores = jnp.einsum('gqd,gkd->gqk', query_f, key_f) * scale
    scores = jnp.where(allowed, scores, -jnp.inf)
    highest = lax.optimization_barrier(jnp.max(scores, axis=-1, keepdims=True))
    expo = jnp.where(allowed, jnp.exp(scores - highest), 0.0)
    probs = expo / lax.optimization_barrier(jnp.sum(expo, axis=-1, keepdims=True))
    probs_b = lax.optimization_barrier(probs.astype(jnp.bfloat16)).astype(jnp.float32)
    output = jnp.einsum('gqk,gkd->gqd', probs_b, value_f)
    output_b = lax.optimization_barrier(output.astype(jnp.bfloat16)).astype(jnp.float32)
    dprob = jnp.einsum('gqd,gkd->gqk', grad_f, value_f)
    delta = lax.optimization_barrier(jnp.sum(grad_f * output_b, axis=-1, keepdims=True))
    dscore = probs * (dprob - delta)
    dscore_b = lax.optimization_barrier((dscore * scale).astype(jnp.bfloat16)).astype(jnp.float32)
    dquery = jnp.einsum('gqk,gkd->gqd', dscore_b, key_f)
    dvalue = jnp.einsum('gqk,gqd->gkd', probs_b, grad_f)

    def restore(tensor):
        return jnp.roll(tensor.reshape(TOKENS, HEAD_DIM), amount, axis=0)
    return (restore(output_b).astype(jnp.bfloat16), restore(dquery), restore(dvalue))

def reference(hidden_states, w_query, w_key, w_value, a_query, a_value, b_query, b_value, positions, out_grad):
    cosine, sine = rope_tables(positions)
    base_q = jnp.dot(hidden_states, w_query, preferred_element_type=jnp.float32)
    base_k = jnp.dot(hidden_states, w_key, preferred_element_type=jnp.float32)
    base_v = jnp.dot(hidden_states, w_value, preferred_element_type=jnp.float32)
    low_q = jnp.dot(hidden_states, a_query, preferred_element_type=jnp.float32).astype(jnp.bfloat16)
    low_v = jnp.dot(hidden_states, a_value, preferred_element_type=jnp.float32).astype(jnp.bfloat16)
    pre_q = base_q + 2.0 * jnp.dot(low_q, b_query, preferred_element_type=jnp.float32)
    queries = rotate(pre_q.reshape(TOKENS, HEADS, HEAD_DIM), cosine, sine).astype(jnp.bfloat16)
    keys = rotate(base_k.reshape(TOKENS, HEADS, HEAD_DIM), cosine, sine).astype(jnp.bfloat16)
    values = (base_v + 2.0 * jnp.dot(low_v, b_value, preferred_element_type=jnp.float32)).astype(jnp.bfloat16)
    values = values.reshape(TOKENS, HEADS, HEAD_DIM)
    grads = out_grad.reshape(TOKENS, HEADS, HEAD_DIM)
    moved = (jnp.arange(HEADS) >= HEADS // 2).astype(jnp.int32)
    outputs, dquery, dvalue = lax.map(head_pass, (queries.transpose(1, 0, 2), keys.transpose(1, 0, 2), values.transpose(1, 0, 2), grads.transpose(1, 0, 2), moved))
    attn_out = outputs.transpose(1, 0, 2).reshape(TOKENS, HD)
    dq = rotate(dquery.transpose(1, 0, 2), cosine, -sine).astype(jnp.bfloat16).reshape(TOKENS, HD)
    dv = dvalue.transpose(1, 0, 2).astype(jnp.bfloat16).reshape(TOKENS, HD)
    grad_b_query = 2.0 * jnp.dot(low_q.T, dq, preferred_element_type=jnp.float32)
    grad_b_value = 2.0 * jnp.dot(low_v.T, dv, preferred_element_type=jnp.float32)
    low_grads = jnp.concatenate([2.0 * jnp.dot(dq, b_query.T, preferred_element_type=jnp.float32), 2.0 * jnp.dot(dv, b_value.T, preferred_element_type=jnp.float32)], axis=1)
    grad_down = lax.dot_general(hidden_states.astype(jnp.float32), low_grads, (((0,), (0,)), ((), ())), precision=lax.Precision.HIGHEST)
    return (attn_out, grad_down[:, :RANK], grad_b_query, grad_down[:, RANK:], grad_b_value)
```

```python
import functools
import math

import jax
import jax.numpy as jnp
from jax import lax
from jax.experimental import pallas as pl
from jax.experimental.pallas import tpu as pltpu
from jax.sharding import PartitionSpec as P

HEAD_DIM = 128
HEADS = 16
TRAIN_CTX = 4096
MAX_POS = 100000


def passed_along(block, axis, distance):
    devices = range(lax.axis_size(axis))
    route = [((i - distance) % len(devices), i) for i in devices]
    return lax.ppermute(block, axis, route)


def rope_tables(positions):
    half_dim = HEAD_DIM // 2
    inverse = jnp.exp(
        jnp.arange(half_dim, dtype=jnp.float32) * (-2.0 * math.log(10000.0) / HEAD_DIM)
    )
    scaled = positions.astype(jnp.float32) * (TRAIN_CTX / MAX_POS)
    angle = scaled[:, None] * inverse[None, :]
    return (jnp.cos(angle)[:, None, :], jnp.sin(angle)[:, None, :])


def rotate(vectors, cosine, sine):
    half_dim = vectors.shape[-1] // 2
    first = vectors[..., :half_dim]
    second = vectors[..., half_dim:]
    return jnp.concatenate(
        [first * cosine - second * sine, second * cosine + first * sine], axis=-1
    )


def project_back(features, low_grads):
    block_width = min(features.shape[1], 512)
    block_count = features.shape[1] // block_width

    def one_block(number):
        section = lax.dynamic_slice_in_dim(features, number * block_width, block_width, 1).astype(
            jnp.float32
        )
        return lax.dot_general(
            section, low_grads, (((0,), (0,)), ((), ())), precision=lax.Precision.HIGHEST
        )

    blocks = lax.map(one_block, jnp.arange(block_count))
    return blocks.reshape(features.shape[1], low_grads.shape[1])


def local(
    hidden_states, w_query, w_key, w_value, a_query, a_value, b_query, b_value, positions, out_grad
):
    rows_here = hidden_states.shape[0]
    columns = w_query.shape[1]
    heads_here = columns // HEAD_DIM
    rank_cols = a_query.shape[1]
    scale = 1.0 / math.sqrt(HEAD_DIM)
    shard_count = lax.axis_size("ctx")
    total_tokens = rows_here * shard_count
    group_len = total_tokens // 4
    reach = (group_len // 2 % rows_here + group_len - 1) // rows_here
    full_states = lax.all_gather(hidden_states, ("head", "sub"), axis=1, tiled=True)
    pieces = (
        lax.all_gather(w_query, "ctx", axis=0, tiled=True),
        lax.all_gather(w_key, "ctx", axis=0, tiled=True),
        lax.all_gather(w_value, "ctx", axis=0, tiled=True),
    )
    base_q, base_k, base_v = tuple(
        (
            jnp.dot(full_states, weights_piece, preferred_element_type=jnp.float32)
            for weights_piece in pieces
        )
    )
    low_q = jnp.dot(full_states, a_query, preferred_element_type=jnp.float32).astype(jnp.bfloat16)
    low_v = jnp.dot(full_states, a_value, preferred_element_type=jnp.float32).astype(jnp.bfloat16)
    cosine, sine = rope_tables(positions)
    pre_q = base_q + 2.0 * jnp.dot(low_q, b_query, preferred_element_type=jnp.float32)
    queries = rotate(pre_q.reshape(rows_here, heads_here, HEAD_DIM), cosine, sine).astype(
        jnp.bfloat16
    )
    keyed = rotate(base_k.reshape(rows_here, heads_here, HEAD_DIM), cosine, sine).astype(
        jnp.bfloat16
    )
    valued = (base_v + 2.0 * jnp.dot(low_v, b_value, preferred_element_type=jnp.float32)).astype(
        jnp.bfloat16
    )
    valued = valued.reshape(rows_here, heads_here, HEAD_DIM)
    current = jnp.stack([keyed, valued])
    collected = [current]
    for level in range(reach):
        current = passed_along(current, "ctx", 1)
        collected.append(current)
    key_rows = jnp.concatenate([block[0] for block in collected], axis=0)
    value_rows = jnp.concatenate([block[1] for block in collected], axis=0)
    shard_id = lax.axis_index("ctx")
    head_ids = lax.axis_index(("head", "sub")) * heads_here + jnp.arange(heads_here)
    amount = jnp.where(head_ids >= HEADS // 2, group_len // 2, 0).astype(jnp.int32)
    query_pos = shard_id * rows_here + jnp.arange(rows_here, dtype=jnp.int32)
    block_ids = jnp.arange(reach + 1, dtype=jnp.int32)
    source_shard = (shard_id - block_ids) % shard_count
    key_pos = (
        source_shard[:, None] * rows_here + jnp.arange(rows_here, dtype=jnp.int32)[None, :]
    ).reshape(-1)
    query_num = (query_pos[None, :] - amount[:, None]) % total_tokens
    key_num = (key_pos[None, :] - amount[:, None]) % total_tokens
    same_group = key_num[:, None, :] // group_len == query_num[:, :, None] // group_len
    visible = same_group & (key_num[:, None, :] <= query_num[:, :, None])
    scores = (
        jnp.einsum("qhd,khd->hqk", queries, key_rows, preferred_element_type=jnp.float32) * scale
    )
    scores = jnp.where(visible, scores, -jnp.inf)
    highest = jnp.max(scores, axis=-1, keepdims=True)
    expo = jnp.where(visible, jnp.exp(scores - highest), 0.0)
    probs = expo / jnp.sum(expo, axis=-1, keepdims=True)
    probs_b = probs.astype(jnp.bfloat16)
    attended = jnp.einsum("hqk,khd->qhd", probs_b, value_rows, preferred_element_type=jnp.float32)
    attn_out = attended.astype(jnp.bfloat16)
    grads = out_grad.reshape(rows_here, heads_here, HEAD_DIM)
    dprob = jnp.einsum("qhd,khd->hqk", grads, value_rows, preferred_element_type=jnp.float32)
    delta = jnp.sum(grads.astype(jnp.float32) * attn_out.astype(jnp.float32), axis=-1)
    dscore = probs * (dprob - delta.T[:, :, None])
    dscore_b = (dscore * scale).astype(jnp.bfloat16)
    dquery = jnp.einsum("hqk,khd->qhd", dscore_b, key_rows, preferred_element_type=jnp.float32)
    dvalue = jnp.einsum("hqk,qhd->khd", probs_b, grads, preferred_element_type=jnp.float32)
    value_blocks = dvalue.reshape(reach + 1, rows_here, columns)
    carried = value_blocks[reach]
    for level in range(reach, 0, -1):
        carried = passed_along(carried, "ctx", -1) + value_blocks[level - 1]
    dv_local = carried.astype(jnp.bfloat16)
    dq_local = rotate(dquery, cosine, -sine).astype(jnp.bfloat16).reshape(rows_here, columns)
    grad_bq = 2.0 * jnp.dot(low_q.T, dq_local, preferred_element_type=jnp.float32)
    grad_bv = 2.0 * jnp.dot(low_v.T, dv_local, preferred_element_type=jnp.float32)
    low_grads = jnp.concatenate(
        [
            2.0 * jnp.dot(dq_local, b_query.T, preferred_element_type=jnp.float32),
            2.0 * jnp.dot(dv_local, b_value.T, preferred_element_type=jnp.float32),
        ],
        axis=1,
    )
    grad_down = lax.psum(project_back(full_states, low_grads), ("ctx", "head", "sub"))
    grad_bq, grad_bv = lax.psum((grad_bq, grad_bv), "ctx")
    return (
        attn_out.reshape(rows_here, columns),
        grad_down[:, :rank_cols],
        grad_bq,
        grad_down[:, rank_cols:],
        grad_bv,
    )


LANES = 128
MESH = pl.DeviceIdType.MESH
NP = 4
WP = 2


def paired_kernel(
    hid_ref,
    wq_ref,
    wk_ref,
    wv_ref,
    aq_ref,
    av_ref,
    bq_ref,
    bv_ref,
    pos_ref,
    og_ref,
    out_ref,
    gaq_ref,
    gbq_ref,
    gav_ref,
    gbv_ref,
    hbuf,
    wbuf,
    relay,
    psend,
    precv,
    lsend,
    lrecv,
    qkv,
    qsend,
    lowt,
    ball,
    ogbuf,
    posbuf,
    ctab,
    stab,
    osend,
    orecv,
    gbs,
    gbr,
    lgacc,
    lgs,
    lgr,
    gas,
    gar,
    local_sem,
    hz_send,
    hxr_send,
    rl_recv,
    hx_send,
    hs_send,
    h_recv,
    w_send,
    wy_send,
    w_recv,
    p_send,
    p_recv,
    l_send,
    l_recv,
    q_send,
    q_recv,
    lq_send,
    lq_recv,
    og_send,
    og_recv,
    pos_send,
    pos_recv,
    o_send,
    o_recv,
    gb_send,
    gb_recv,
    lg_send,
    lg_recv,
    ga_send,
    ga_recv,
):
    f32, bf16 = jnp.float32, jnp.bfloat16
    rows, width = hid_ref.shape
    depth = wq_ref.shape[0]
    hl = rows // 2
    pr = hl // NP
    wrows = depth // (2 * WP)
    chunks = 2 * 4
    slice_k = 2 * width // 4
    r, c = lax.axis_index("rep"), lax.axis_index("ctx")
    h, s = lax.axis_index("head"), lax.axis_index("sub")
    m = c // 2
    inner = (c == 1) | (c == 2)
    outer = (c == 0) | (c == 3)
    near = 1 + m
    far_c = 3 - c
    rim = 3 * m
    home = h == m
    away = h != m
    me = c * 4 + h * 2 + s
    weights = (wq_ref, wk_ref, wv_ref)
    dot_t = functools.partial(
        lax.dot_general, dimension_numbers=(((1,), (1,)), ((), ())), preferred_element_type=f32
    )
    t_dot = functools.partial(
        lax.dot_general, dimension_numbers=(((0,), (0,)), ((), ())), preferred_element_type=f32
    )

    def member(number):
        hs = lax.rem(number, 4)
        return {"ctx": number // 4, "head": hs // 2, "sub": lax.rem(hs, 2)}

    def remote(src, dst, send, recv, device):
        return pltpu.make_async_remote_copy(
            src_ref=src, dst_ref=dst, send_sem=send, recv_sem=recv, device_id=device, device_id_type=MESH
        )

    def rows_at(start, size):
        return pl.ds(pl.multiple_of(start, 16), size)

    def cols(number, size):
        return pl.ds(pl.multiple_of(number * size, LANES), size)

    barrier = pltpu.get_barrier_semaphore()
    for k in range(1, 16):
        pl.semaphore_signal(barrier, inc=1, device_id=member(lax.rem(me + k, 16)), device_id_type=MESH)
    pl.semaphore_signal(barrier, inc=1, device_id={"rep": 1 - r}, device_id_type=MESH)

    def own_piece(e, p):
        return hid_ref.at[pl.ds(e * hl + p * pr, pr), :]

    def chunk_of(b, e, hd):
        return lax.rem(2 * b + e - hd + chunks, chunks)

    def hslot(b, e, p, hd, q):
        return hbuf.at[rows_at(chunk_of(b, e, hd) * hl + p * pr, pr), cols(q, width)]

    def wslot(j, t, quarter, side, w):
        return wbuf.at[j, t, rows_at(quarter * depth + side * (depth // 2) + w * wrows, wrows), :]

    own_h = [
        pltpu.make_async_copy(
            hid_ref.at[pl.ds(e * hl, hl), :],
            hbuf.at[rows_at(chunk_of(c, e, h) * hl, hl), cols(s, width)],
            local_sem.at[e],
        )
        for e in range(2)
    ]
    own_pos = pltpu.make_async_copy(pos_ref, posbuf.at[c], local_sem.at[2])
    own_og = [
        pltpu.make_async_copy(og_ref.at[pl.ds(0, hl), :], ogbuf.at[pl.ds(0, hl), :], local_sem.at[3]),
        pltpu.make_async_copy(
            og_ref.at[pl.ds(hl, hl), :], ogbuf.at[rows_at(hl - h * hl, hl), :], local_sem.at[4]
        ),
    ]

    def own_w(j, t):
        return pltpu.make_async_copy(
            weights[t].at[:, pl.ds(j * LANES, LANES)],
            wbuf.at[j, t, rows_at((c - 2 * m) * depth, depth), :],
            local_sem.at[5 + 3 * j + t],
        )

    own_pos.start()

    @pl.when(inner & home)
    def _():
        for copy in own_h:
            copy.start()

    @pl.when(inner)
    def _():
        for j in range(4):
            for t in range(3):
                own_w(j, t).start()

    own_og[1].start()
    pl.when(h == 0)(own_og[0].start)
    pl.semaphore_wait(barrier, 16)

    def h_direct(p):
        return remote(own_piece(1, p), hslot(c, 1, p, h, s), hz_send.at[0, p], h_recv.at[c, 1, p, s], {"ctx": 1 + h})

    def h_relay_in(p):
        return remote(
            own_piece(0, p), relay.at[pl.ds(p * pr, pr), :], hxr_send.at[p], rl_recv.at[p], {"head": 1 - h}
        )

    def h_relay_out(p):
        return remote(
            relay.at[pl.ds(p * pr, pr), :],
            hslot(c, 0, p, h, s),
            hz_send.at[1, p],
            h_recv.at[c, 0, p, s],
            {"ctx": 2 - h},
        )

    direct_on = c != 1 + h
    relay_on = c != 2 - h

    def h_cross(b, e, p, src=None):
        return remote(
            hslot(b, e, p, h, s) if src is None else src,
            hslot(b, e, p, 1 - h, s),
            hx_send.at[b, e, p],
            h_recv.at[b, e, p, s],
            {"head": 1 - h},
        )

    def h_twin(b, e, p, src=None):
        land = hslot(b, e, p, h, s)
        return remote(
            land if src is None else src, land, hs_send.at[b, e, p], h_recv.at[b, e, p, s], {"sub": 1 - s}
        )

    def h_arrived(b, e, p, q):
        land = hslot(b, e, p, h, q)
        return remote(land, land, hx_send.at[0, 0, 0], h_recv.at[b, e, p, q], {"sub": 1 - s})

    def w_out(j, t, w):
        return remote(
            weights[t].at[rows_at(r * (depth // 2) + w * wrows, wrows), pl.ds(j * LANES, LANES)],
            wslot(j, t, c - 2 * m, r, w),
            w_send.at[j, t, w],
            w_recv.at[j, t, r, w],
            {"ctx": near},
        )

    other = 1 - (c - 2 * m)

    def w_pass(j, t, w):
        land = wslot(j, t, other, r, w)
        return remote(land, land, wy_send.at[j, t, w], w_recv.at[j, t, r, w], {"rep": 1 - r})

    def w_arrived(j, t, w):
        land = wslot(j, t, other, 1 - r, w)
        return remote(land, land, wy_send.at[0, 0, 0], w_recv.at[j, t, 1 - r, w], {"rep": 1 - r})

    def p_out(j, t, g):
        return remote(
            psend.at[j, t, g], precv.at[j, t, g], p_send.at[j, t, g], p_recv.at[j, t, g], {"ctx": 3 - c}
        )

    def l_out(g):
        return remote(lsend.at[g], lrecv.at[g], l_send.at[g], l_recv.at[g], {"ctx": 3 - c})

    def q_out(j, t):
        return remote(qsend.at[j, t], qkv.at[j, t], q_send.at[j, t], q_recv.at[j, t], {"ctx": rim})

    lq_out = remote(lowt.at[1], lowt.at[0], lq_send.at[0], lq_recv.at[0], {"ctx": rim})
    og_out = remote(
        og_ref.at[pl.ds(0, hl), :], ogbuf.at[pl.ds(hl, hl), :], og_send.at[0], og_recv.at[0], {"ctx": lax.rem(c + 3, 4)}
    )

    def pos_out(k):
        return remote(pos_ref, posbuf.at[c], pos_send.at[k - 1], pos_recv.at[c], {"ctx": lax.rem(c + k, 4)})

    def o_out(j):
        return remote(osend.at[j], orecv.at[j], o_send.at[j], o_recv.at[j], {"ctx": lax.rem(c + 1, 4)})

    def gb_out(j, k):
        return remote(gbs.at[j], gbr.at[c, j], gb_send.at[j, k - 1], gb_recv.at[j, c], {"ctx": lax.rem(c + k, 4)})

    def tables():
        for block in range(4):

            @pl.when(block != c)
            def _():
                remote(pos_ref, posbuf.at[block], pos_send.at[0], pos_recv.at[block], {"sub": 1 - s}).wait_recv()

        own_pos.wait()
        lane = lax.broadcasted_iota(jnp.int32, (LANES, LANES), 1)
        half_dim = LANES // 2
        index = lax.broadcasted_iota(jnp.int32, (8, LANES), 1) % half_dim
        inverse = jnp.exp(index.astype(f32) * (-2.0 * math.log(10000.0) / HEAD_DIM))[0:1, :]

        def one(number, carry):
            place = lax.rem(4 * m + number + h, chunks)
            row = posbuf[place // 2, pl.ds(lax.rem(place, 2), 1), :].astype(f32)
            column = jnp.transpose(jnp.broadcast_to(row, (LANES, LANES)))
            angle = (column * (TRAIN_CTX / MAX_POS)) * inverse
            here = pl.ds(pl.multiple_of(number * LANES, LANES), LANES)
            ctab[here, :] = jnp.cos(angle)
            sine = jnp.sin(angle)
            stab[here, :] = jnp.where(lane < LANES // 2, -sine, sine)
            return carry

        lax.fori_loop(0, 4, one, 0)

    def turn(u, cosine, sine):
        return u * cosine + pltpu.roll(u, LANES // 2, 1) * sine

    nothing = jnp.zeros((8, 4 * LANES), f32)
    ball[0] = jnp.concatenate([bq_ref[...].astype(f32), nothing], axis=0).astype(bf16)
    ball[1] = jnp.concatenate([nothing, nothing], axis=0).astype(bf16)
    ball[2] = jnp.concatenate([nothing, bv_ref[...].astype(f32)], axis=0).astype(bf16)
    lgacc[...] = jnp.zeros(lgacc.shape, f32)

    scale = 1.0 / math.sqrt(HEAD_DIM)
    mine = rows_at((c - 2 * m) * rows, rows)

    def attend(j):
        here = cols(j, LANES)
        q, k, v, grad = qkv[j, 0], qkv[j, 1], qkv[j, 2], ogbuf[:, here]
        allowed = lax.broadcasted_iota(jnp.int32, (rows, rows), 0) >= lax.broadcasted_iota(
            jnp.int32, (rows, rows), 1
        )
        scores = jnp.where(allowed, dot_t(q, k) * scale, -jnp.inf)
        highest = jnp.max(scores, axis=-1, keepdims=True)
        expo = jnp.where(allowed, jnp.exp(scores - highest), 0.0)
        probs = expo / jnp.sum(expo, axis=-1, keepdims=True)
        probs_b = probs.astype(bf16)
        out = jnp.dot(probs_b, v, preferred_element_type=f32).astype(bf16)
        osend[j] = out[hl:]

        @pl.when(h == 0)
        def _():
            out_ref[:, here] = out

        @pl.when(h == 1)
        def _():
            o_out(j).start()
            out_ref[pl.ds(hl, hl), here] = out[:hl]

        dprob = dot_t(grad, v)
        delta = jnp.sum(grad.astype(f32) * out.astype(f32), axis=-1, keepdims=True)
        dscore_b = (probs * (dprob - delta) * scale).astype(bf16)
        dq = jnp.dot(dscore_b, k, preferred_element_type=f32)
        dq = turn(dq, ctab[mine, :], -stab[mine, :]).astype(bf16)
        dv = t_dot(probs_b, grad).astype(bf16)
        lgacc[...] += 2.0 * (dot_t(ball[0, :, here], dq) + dot_t(ball[2, :, here], dv))
        low = lowt[0]
        gbs[j, 0:8, :] = (2.0 * jnp.dot(low, dq, preferred_element_type=f32))[0:8]
        gbs[j, 8:16, :] = (2.0 * jnp.dot(low, dv, preferred_element_type=f32))[8:16]
        for k_ in range(1, 4):
            gb_out(j, k_).start()

    for k in range(1, 4):
        pos_out(k).start()

    def og_in():
        @pl.when(h == 1)
        def _():
            og_out.wait_recv()
            own_og[1].wait()

        @pl.when(h == 0)
        def _():
            own_og[0].wait()
            own_og[1].wait()

    @pl.when(inner)
    def _():
        e = jnp.where(home, 1, 0)

        @pl.when(home)
        def _():
            for half in range(2):
                for p in range(NP):
                    h_twin(c, half, p, own_piece(half, p)).start()

        @pl.when(away)
        def _():
            for p in range(NP):
                h_relay_in(p).start()
                h_direct(p).start()

        def z_in(b, p):
            h_arrived(b, e, p, s).wait_recv()
            h_cross(b, e, p).start()
            h_twin(b, e, p).start()

        def x_in(b, half, p):
            h_arrived(b, half, p, s).wait_recv()
            h_twin(b, half, p).start()

        def twin_in(b):
            for half in range(2):
                for p in range(NP):
                    h_arrived(b, half, p, 1 - s).wait_recv()

        def forward(j, t):
            for w in range(WP):
                copy = w_pass(j, t, w)
                copy.wait_recv()
                copy.start()

        def passed(j, t):
            for w in range(WP):
                w_arrived(j, t, w).wait_recv()

        def group_rows(g):
            return rows_at(g * rows, rows)

        def partner(j, t, g):
            group = jnp.where(g == 0, 3 - c, 3 * (1 - m))
            y = jnp.dot(hbuf[group_rows(group), :], wbuf[j, t], preferred_element_type=f32)
            psend[j, t, g] = y.astype(bf16)
            p_out(j, t, g).start()

        whole = [(half, p) for half in range(2) for p in range(NP)]
        pieces = [(t, w) for t in range(3) for w in range(WP)]
        rest = list(pieces)

        def forward_piece(j, t, w):
            copy = w_pass(j, t, w)
            copy.wait_recv()
            copy.start()

        for p in range(NP):

            @pl.when(home)
            def _():
                h_relay_in(p).wait_recv()
                h_relay_out(p).start()

            z_in(3 - c, p)
            forward_piece(0, *rest.pop(0))
        tables()

        @pl.when(home)
        def _():
            for half, p in whole[:2]:
                h_cross(c, half, p, own_piece(half, p)).start()

        while rest:
            forward_piece(0, *rest.pop(0))
        pl.when(h == 1)(og_out.start)
        far = 3 * (1 - m)
        late = (c == 1) & (h == 1)

        def first_in(t, carry):
            partner(0, t, 0)
            return carry

        def first_out(t, carry):
            partner(0, t, 1)
            return carry

        for p in range(NP // 2):
            z_in(far, p)
        for p in range(NP):
            x_in(3 - c, 1 - e, p)
            if p + NP // 2 < NP - 1:
                z_in(far, p + NP // 2)
        twin_in(3 - c)

        @pl.when(home)
        def _():
            for copy in own_h:
                copy.wait()
            twin_in(c)

        for t in range(3):
            own_w(0, t).wait()
            passed(0, t)

        @pl.when(jnp.logical_not(late))
        def _():
            lax.fori_loop(0, 3, first_in, 0)

        z_in(far, NP - 1)
        for p in range(NP):
            z_in(rim, p)
            x_in(far, 1 - e, p)

        @pl.when(home)
        def _():
            for half, p in whole[2:]:
                h_cross(c, half, p, own_piece(half, p)).start()

        twin_in(far)

        @pl.when(late)
        def _():
            lax.fori_loop(0, 3, first_in, 0)

        forward(1, 0)
        for p in range(NP):
            x_in(rim, 1 - e, p)
        twin_in(rim)
        lax.fori_loop(0, 3, first_out, 0)
        for j in range(1, 4):
            for t in range(3):
                own_w(j, t).wait()
        a_both = jnp.concatenate(
            [
                aq_ref[:, pl.ds(pl.multiple_of(m * 2 * width, LANES), 2 * width)].astype(f32),
                av_ref[:, pl.ds(pl.multiple_of(m * 2 * width, LANES), 2 * width)].astype(f32),
            ],
            axis=0,
        ).astype(bf16)

        def low_other(g, carry):
            group = jnp.where(g == 0, 3 - c, 3 * (1 - m))
            lsend[g] = dot_t(a_both, hbuf[group_rows(group), :])
            l_out(g).start()
            return carry

        forward(1, 1)
        lax.fori_loop(0, 2, low_other, 0)

        def low_own(g, carry):
            group = jnp.where(g == 0, c, rim)
            l_out(g).wait_recv()
            lowt[g] = (dot_t(a_both, hbuf[group_rows(group), :]) + lrecv[g]).astype(bf16)
            return carry

        def finish(i):
            j, t = i // 3, lax.rem(i, 3)
            plain = t == 2

            def one(step, carry):
                g = 1 - step
                group = jnp.where(g == 0, c, rim)
                y = jnp.dot(hbuf[group_rows(group), :], wbuf[j, t], preferred_element_type=f32)
                up = 2.0 * t_dot(lowt[g], ball[t, :, cols(j, LANES)])
                p_out(j, t, g).wait_recv()
                y = y + precv[j, t, g].astype(f32) + up
                there = rows_at(jnp.where(g == 0, c - 2 * m, m) * rows, rows)
                cosine = jnp.where(plain, 1.0, ctab[there, :])
                sine = jnp.where(plain, 0.0, stab[there, :])
                y = turn(y, cosine, sine).astype(bf16)

                @pl.when(g == 1)
                def _():
                    qsend[j, t] = y
                    q_out(j, t).start()

                @pl.when(g == 0)
                def _():
                    qkv[j, t] = y

                return carry

            lax.fori_loop(0, 2, one, 0)

        def slot(i, carry):
            @pl.when(i < 13)
            def _():
                j, t = (i - 1) // 3, lax.rem(i - 1, 3)
                passed(j, t)

                def one(step, carry_):
                    partner(j, t, 1 - step)
                    return carry_

                lax.fori_loop(0, 2, one, 0)

            @pl.when(i < 11)
            def _():
                forward((i + 1) // 3, lax.rem(i + 1, 3))

            @pl.when(i == 6)
            def _():
                @pl.when(away)
                def _():
                    for half, p in whole:
                        x_in(c, half, p)
                    twin_in(c)

                lax.fori_loop(0, 2, low_own, 0)
                lq_out.start()
                og_in()

            first = jnp.where(i == 6, 0, jnp.where(i == 7, 2, i - 4))
            count = jnp.where(i < 6, 0, jnp.where(i < 8, 2, 1))

            def some(k, carry_):
                finish(first + k)
                return carry_

            lax.fori_loop(0, count, some, 0)

            @pl.when((i == 7) | (i == 9) | (i == 12) | (i == 15))
            def _():
                attend(jnp.where(i == 15, 3, (i - 6) // 2 - jnp.where(i == 12, 1, 0)))

            return carry

        lax.fori_loop(4, 16, slot, 0)

    @pl.when(outer)
    def _():
        for t in range(3):
            for w in range(WP):
                w_out(0, t, w).start()
        for p in range(NP):
            h_relay_in(p).start()

        def relays():
            for p in range(NP):
                h_relay_in(p).wait_recv()
                h_relay_out(p).start()

        @pl.when(home)
        def _():
            relays()
            for p in range(NP):
                h_direct(p).start()

        @pl.when(away)
        def _():
            for p in range(NP):
                h_direct(p).start()
            relays()

        def send_w(j, carry):
            for t in range(3):
                for w in range(WP):
                    remote(
                        weights[t].at[rows_at(r * (depth // 2) + w * wrows, wrows), cols(j, LANES)],
                        wslot(j, t, c - 2 * m, r, w),
                        w_send.at[j, t, w],
                        w_recv.at[j, t, r, w],
                        {"ctx": near},
                    ).start()
            return carry

        lax.fori_loop(1, 4, send_w, 0)
        pl.when(h == 1)(og_out.start)
        tables()
        og_in()
        remote(lowt.at[0], lowt.at[0], lq_send.at[0], lq_recv.at[0], {"sub": 1 - s}).wait_recv()

        def one(j, carry):
            for t in range(3):
                q_out(j, t).wait_recv()
            attend(j)
            return carry

        lax.fori_loop(0, 4, one, 0)

    lgs[...] = lgacc[...].astype(bf16)
    lgr[me] = lgs[...]

    def lg_out(k):
        dest = 4 + k
        return remote(lgs, lgr.at[me], lg_send.at[k], lg_recv.at[me], member(dest))

    for k in range(8):
        pl.when(me != 4 + k)(lg_out(k).start)

    def ga_out(k):
        dest = lax.rem(me + k, 16)
        return remote(gas, gar.at[me - 4], ga_send.at[k - 1], ga_recv.at[me - 4], member(dest))

    @pl.when(inner)
    def _():
        for k in range(1, 16):
            frm = lax.rem(me + k, 16)
            remote(lgs, lgr.at[frm], lg_send.at[0], lg_recv.at[frm], {"sub": 1 - s}).wait_recv()

        def side(hd):
            return jnp.concatenate(
                [
                    lgr[4 * g + 2 * hd].astype(f32) + lgr[4 * g + 2 * hd + 1].astype(f32)
                    for g in range(4)
                ],
                axis=1,
            )

        zero, one = side(0), side(1)
        wide_ = 4 * rows
        right = jnp.concatenate([one[:, wide_ - hl :], one[:, : wide_ - hl]], axis=1)
        left = jnp.concatenate([zero[:, hl:], zero[:, :hl]], axis=1)
        low = jnp.where(h == 0, zero + right, left + one)
        upper = low.astype(bf16)
        lower = (low - upper.astype(f32)).astype(bf16)
        both = jnp.concatenate([upper, lower], axis=0)
        part_ = jnp.dot(both, hbuf[:, cols(h * 2 + s, slice_k)], preferred_element_type=f32)
        gas[...] = (part_[0:16] + part_[16:32]).astype(bf16)
        gar[me - 4] = gas[...]
        for k in range(1, 16):
            ga_out(k).start()

    @pl.when(h == 1)
    def _():
        for j in range(4):
            o_out(j).wait_recv()
            out_ref[0:hl, j * LANES : (j + 1) * LANES] = orecv[j]

    for j in range(4):
        for block in range(4):

            @pl.when(block != c)
            def _():
                remote(gbs.at[0], gbr.at[block, j], gb_send.at[0, 0], gb_recv.at[j, block], {"sub": 1 - s}).wait_recv()

        gbr[c, j] = gbs[j]
        total = (gbr[0, j] + gbr[1, j]) + (gbr[2, j] + gbr[3, j])
        gbq_ref[:, j * LANES : (j + 1) * LANES] = total[0:8]
        gbv_ref[:, j * LANES : (j + 1) * LANES] = total[8:16]

    for k in range(8):

        @pl.when(me != 4 + k)
        def _():
            remote(gas, gar.at[k], ga_send.at[0], ga_recv.at[k], {"sub": 1 - s}).wait_recv()

        block = gar[k].astype(f32)
        gaq_ref[:, k * slice_k : (k + 1) * slice_k] = block[0:8]
        gav_ref[:, k * slice_k : (k + 1) * slice_k] = block[8:16]

    for p in range(NP):
        pl.when(direct_on)(h_direct(p).wait_send)
        pl.when(direct_on)(h_relay_in(p).wait_send)
        pl.when(relay_on)(h_relay_out(p).wait_send)
    for k in range(1, 4):
        pos_out(k).wait_send()

    @pl.when(h == 1)
    def _():
        og_out.wait_send()
        for j in range(4):
            o_out(j).wait_send()

    for j in range(4):
        for k in range(1, 4):
            gb_out(j, k).wait_send()
    for k in range(8):
        pl.when(me != 4 + k)(lg_out(k).wait_send)

    @pl.when(outer)
    def _():
        for j in range(4):
            for t in range(3):
                for w in range(WP):
                    w_out(j, t, w).wait_send()

    @pl.when(inner)
    def _():
        for b in range(4):
            for half in range(2):
                for p in range(NP):
                    h_twin(b, half, p).wait_send()
                    crossed = ((b == c) & home) | ((b != c) & (home == (half == 1)))
                    pl.when(crossed)(h_cross(b, half, p).wait_send)
        for j in range(4):
            for t in range(3):
                for w in range(WP):
                    w_pass(j, t, w).wait_send()
                for g in range(2):
                    p_out(j, t, g).wait_send()
                q_out(j, t).wait_send()
        for g in range(2):
            l_out(g).wait_send()
        lq_out.wait_send()
        for k in range(1, 16):
            ga_out(k).wait_send()


def hand_over_kernel(count, *refs):
    sources, results, stages, sems = refs[:count], refs[count : 2 * count], refs[2 * count : 3 * count], refs[-1]
    fetched = [pltpu.make_async_copy(sources[k], stages[k], sems.at[0, k]) for k in range(count)]
    stored = [pltpu.make_async_copy(stages[k], results[k], sems.at[1, k]) for k in range(count)]
    for copy in fetched:
        copy.start()
    for k in reversed(range(count)):
        fetched[k].wait()
        stored[k].start()
    for copy in stored:
        copy.wait()


def hand_over(*arrays):
    spec = pl.BlockSpec(memory_space=pl.ANY)
    count = len(arrays)
    return pl.pallas_call(
        functools.partial(hand_over_kernel, count),
        out_shape=tuple(jax.ShapeDtypeStruct(a.shape, a.dtype) for a in arrays),
        in_specs=[spec] * count,
        out_specs=[spec] * count,
        scratch_shapes=[pltpu.VMEM(a.shape, a.dtype) for a in arrays] + [pltpu.SemaphoreType.DMA((2, count))],
    )(*arrays)


def paired(
    hidden_states, w_query, w_key, w_value, a_query, a_value, b_query, b_value, positions, out_grad
):
    f32, bf16 = jnp.float32, jnp.bfloat16
    rows, width = hidden_states.shape
    model, rank = a_query.shape
    depth, columns = w_query.shape
    pos = positions.reshape(rows // LANES, LANES)
    vmem, dma = pltpu.VMEM, pltpu.SemaphoreType.DMA
    hbm_spec = pl.BlockSpec(memory_space=pl.ANY)
    vmem_spec = pl.BlockSpec(memory_space=pltpu.VMEM)
    out, gaq, gbq, gav, gbv = pl.pallas_call(
        paired_kernel,
        out_shape=(
            jax.ShapeDtypeStruct((rows, columns), bf16),
            jax.ShapeDtypeStruct((rank, model), f32),
            jax.ShapeDtypeStruct((rank, columns), f32),
            jax.ShapeDtypeStruct((rank, model), f32),
            jax.ShapeDtypeStruct((rank, columns), f32),
        ),
        in_specs=[hbm_spec] * 4 + [vmem_spec] * 4 + [hbm_spec] * 2,
        out_specs=[vmem_spec] * 5,
        scratch_shapes=[
            vmem((4 * rows, 2 * width), bf16),
            vmem((4, 3, 2 * depth, LANES), bf16),
            vmem((rows // 2, width), bf16),
            vmem((4, 3, 2, rows, LANES), bf16),
            vmem((4, 3, 2, rows, LANES), bf16),
            vmem((2, 16, rows), f32),
            vmem((2, 16, rows), f32),
            vmem((4, 3, rows, LANES), bf16),
            vmem((4, 3, rows, LANES), bf16),
            vmem((2, 16, rows), bf16),
            vmem((3, 16, columns), bf16),
            vmem((rows, columns), bf16),
            vmem((4, rows // LANES, LANES), jnp.int32),
            vmem((2 * rows, LANES), f32),
            vmem((2 * rows, LANES), f32),
            vmem((4, rows // 2, LANES), bf16),
            vmem((4, rows // 2, LANES), bf16),
            vmem((4, 16, LANES), f32),
            vmem((4, 4, 16, LANES), f32),
            vmem((16, rows), f32),
            vmem((16, rows), bf16),
            vmem((16, 16, rows), bf16),
            vmem((16, model // 8), bf16),
            vmem((8, 16, model // 8), bf16),
            dma((17,)),
            dma((2, NP)),
            dma((NP,)),
            dma((NP,)),
            dma((4, 2, NP)),
            dma((4, 2, NP)),
            dma((4, 2, NP, 2)),
            dma((4, 3, WP)),
            dma((4, 3, WP)),
            dma((4, 3, 2, WP)),
            dma((4, 3, 2)),
            dma((4, 3, 2)),
            dma((2,)),
            dma((2,)),
            dma((4, 3)),
            dma((4, 3)),
            dma((1,)),
            dma((1,)),
            dma((1,)),
            dma((1,)),
            dma((3,)),
            dma((4,)),
            dma((4,)),
            dma((4,)),
            dma((4, 3)),
            dma((4, 4)),
            dma((8,)),
            dma((16,)),
            dma((15,)),
            dma((8,)),
        ],
        compiler_params=pltpu.CompilerParams(
            collective_id=1, has_side_effects=True, vmem_limit_bytes=56 * 1024 * 1024
        ),
    )(
        hidden_states, w_query, w_key, w_value, a_query.T, a_value.T, b_query, b_value, pos, out_grad
    )
    out, gaq, gbq, gav, gbv = hand_over(out, gaq, gbq, gav, gbv)
    return (out, gaq.T, gbq, gav.T, gbv)


def fits_paired(mesh, args):
    hidden_states, w_query, a_query = args[0], args[1], args[4]
    return (
        mesh.shape["rep"] == 2
        and mesh.shape["ctx"] == 4
        and mesh.shape["head"] == 2
        and mesh.shape["sub"] == 2
        and w_query.shape[1] == 4 * HEAD_DIM
        and HEAD_DIM == LANES
        and HEADS == 16
        and a_query.shape[1] == 8
        and hidden_states.shape[0] == 2 * LANES
        and hidden_states.shape[1] == w_query.shape[0]
        and a_query.shape[0] == 4 * w_query.shape[0]
        and w_query.shape[0] == 1024
    )


def choose(mesh, *args):
    return paired(*args) if fits_paired(mesh, args) else local(*args)


def solution(mesh):
    in_specs = (
        P(("rep", "ctx"), ("head", "sub")),
        P("ctx", ("head", "sub")),
        P("ctx", ("head", "sub")),
        P("ctx", ("head", "sub")),
        P(),
        P(),
        P(None, ("head", "sub")),
        P(None, ("head", "sub")),
        P(("rep", "ctx")),
        P(("rep", "ctx"), ("head", "sub")),
    )
    out_specs = (
        P(("rep", "ctx"), ("head", "sub")),
        P(None, "rep"),
        P("rep", ("head", "sub")),
        P(None, "rep"),
        P("rep", ("head", "sub")),
    )
    return jax.shard_map(
        functools.partial(choose, mesh), mesh=mesh, in_specs=in_specs, out_specs=out_specs, check_vma=False
    )
```

```python
import functools
import math

import jax
import jax.numpy as jnp
from jax import lax
from jax.experimental import pallas as pl
from jax.experimental.pallas import tpu as pltpu
from jax.sharding import PartitionSpec as P

HEAD_DIM = 128
HEADS = 16
TRAIN_CTX = 4096
MAX_POS = 100000


def passed_along(block, axis, distance):
    devices = range(lax.axis_size(axis))
    route = [((i - distance) % len(devices), i) for i in devices]
    return lax.ppermute(block, axis, route)


def rope_tables(positions):
    half_dim = HEAD_DIM // 2
    inverse = jnp.exp(
        jnp.arange(half_dim, dtype=jnp.float32) * (-2.0 * math.log(10000.0) / HEAD_DIM)
    )
    scaled = positions.astype(jnp.float32) * (TRAIN_CTX / MAX_POS)
    angle = scaled[:, None] * inverse[None, :]
    return (jnp.cos(angle)[:, None, :], jnp.sin(angle)[:, None, :])


def rotate(vectors, cosine, sine):
    half_dim = vectors.shape[-1] // 2
    first = vectors[..., :half_dim]
    second = vectors[..., half_dim:]
    return jnp.concatenate(
        [first * cosine - second * sine, second * cosine + first * sine], axis=-1
    )


def project_back(features, low_grads):
    block_width = min(features.shape[1], 512)
    block_count = features.shape[1] // block_width

    def one_block(number):
        section = lax.dynamic_slice_in_dim(features, number * block_width, block_width, 1).astype(
            jnp.float32
        )
        return lax.dot_general(
            section, low_grads, (((0,), (0,)), ((), ())), precision=lax.Precision.HIGHEST
        )

    blocks = lax.map(one_block, jnp.arange(block_count))
    return blocks.reshape(features.shape[1], low_grads.shape[1])


def local(
    hidden_states, w_query, w_key, w_value, a_query, a_value, b_query, b_value, positions, out_grad
):
    rows_here = hidden_states.shape[0]
    columns = w_query.shape[1]
    heads_here = columns // HEAD_DIM
    rank_cols = a_query.shape[1]
    scale = 1.0 / math.sqrt(HEAD_DIM)
    shard_count = lax.axis_size("ctx")
    total_tokens = rows_here * shard_count
    group_len = total_tokens // 4
    reach = (group_len // 2 % rows_here + group_len - 1) // rows_here
    full_states = lax.all_gather(hidden_states, ("head", "sub"), axis=1, tiled=True)
    pieces = (
        lax.all_gather(w_query, "ctx", axis=0, tiled=True),
        lax.all_gather(w_key, "ctx", axis=0, tiled=True),
        lax.all_gather(w_value, "ctx", axis=0, tiled=True),
    )
    base_q, base_k, base_v = tuple(
        (
            jnp.dot(full_states, weights_piece, preferred_element_type=jnp.float32)
            for weights_piece in pieces
        )
    )
    low_q = jnp.dot(full_states, a_query, preferred_element_type=jnp.float32).astype(jnp.bfloat16)
    low_v = jnp.dot(full_states, a_value, preferred_element_type=jnp.float32).astype(jnp.bfloat16)
    cosine, sine = rope_tables(positions)
    pre_q = base_q + 2.0 * jnp.dot(low_q, b_query, preferred_element_type=jnp.float32)
    queries = rotate(pre_q.reshape(rows_here, heads_here, HEAD_DIM), cosine, sine).astype(
        jnp.bfloat16
    )
    keyed = rotate(base_k.reshape(rows_here, heads_here, HEAD_DIM), cosine, sine).astype(
        jnp.bfloat16
    )
    valued = (base_v + 2.0 * jnp.dot(low_v, b_value, preferred_element_type=jnp.float32)).astype(
        jnp.bfloat16
    )
    valued = valued.reshape(rows_here, heads_here, HEAD_DIM)
    current = jnp.stack([keyed, valued])
    collected = [current]
    for level in range(reach):
        current = passed_along(current, "ctx", 1)
        collected.append(current)
    key_rows = jnp.concatenate([block[0] for block in collected], axis=0)
    value_rows = jnp.concatenate([block[1] for block in collected], axis=0)
    shard_id = lax.axis_index("ctx")
    head_ids = lax.axis_index(("head", "sub")) * heads_here + jnp.arange(heads_here)
    amount = jnp.where(head_ids >= HEADS // 2, group_len // 2, 0).astype(jnp.int32)
    query_pos = shard_id * rows_here + jnp.arange(rows_here, dtype=jnp.int32)
    block_ids = jnp.arange(reach + 1, dtype=jnp.int32)
    source_shard = (shard_id - block_ids) % shard_count
    key_pos = (
        source_shard[:, None] * rows_here + jnp.arange(rows_here, dtype=jnp.int32)[None, :]
    ).reshape(-1)
    query_num = (query_pos[None, :] - amount[:, None]) % total_tokens
    key_num = (key_pos[None, :] - amount[:, None]) % total_tokens
    same_group = key_num[:, None, :] // group_len == query_num[:, :, None] // group_len
    visible = same_group & (key_num[:, None, :] <= query_num[:, :, None])
    scores = (
        jnp.einsum("qhd,khd->hqk", queries, key_rows, preferred_element_type=jnp.float32) * scale
    )
    scores = jnp.where(visible, scores, -jnp.inf)
    highest = jnp.max(scores, axis=-1, keepdims=True)
    expo = jnp.where(visible, jnp.exp(scores - highest), 0.0)
    probs = expo / jnp.sum(expo, axis=-1, keepdims=True)
    probs_b = probs.astype(jnp.bfloat16)
    attended = jnp.einsum("hqk,khd->qhd", probs_b, value_rows, preferred_element_type=jnp.float32)
    attn_out = attended.astype(jnp.bfloat16)
    grads = out_grad.reshape(rows_here, heads_here, HEAD_DIM)
    dprob = jnp.einsum("qhd,khd->hqk", grads, value_rows, preferred_element_type=jnp.float32)
    delta = jnp.sum(grads.astype(jnp.float32) * attn_out.astype(jnp.float32), axis=-1)
    dscore = probs * (dprob - delta.T[:, :, None])
    dscore_b = (dscore * scale).astype(jnp.bfloat16)
    dquery = jnp.einsum("hqk,khd->qhd", dscore_b, key_rows, preferred_element_type=jnp.float32)
    dvalue = jnp.einsum("hqk,qhd->khd", probs_b, grads, preferred_element_type=jnp.float32)
    value_blocks = dvalue.reshape(reach + 1, rows_here, columns)
    carried = value_blocks[reach]
    for level in range(reach, 0, -1):
        carried = passed_along(carried, "ctx", -1) + value_blocks[level - 1]
    dv_local = carried.astype(jnp.bfloat16)
    dq_local = rotate(dquery, cosine, -sine).astype(jnp.bfloat16).reshape(rows_here, columns)
    grad_bq = 2.0 * jnp.dot(low_q.T, dq_local, preferred_element_type=jnp.float32)
    grad_bv = 2.0 * jnp.dot(low_v.T, dv_local, preferred_element_type=jnp.float32)
    low_grads = jnp.concatenate(
        [
            2.0 * jnp.dot(dq_local, b_query.T, preferred_element_type=jnp.float32),
            2.0 * jnp.dot(dv_local, b_value.T, preferred_element_type=jnp.float32),
        ],
        axis=1,
    )
    grad_down = lax.psum(project_back(full_states, low_grads), ("ctx", "head", "sub"))
    grad_bq, grad_bv = lax.psum((grad_bq, grad_bv), "ctx")
    return (
        attn_out.reshape(rows_here, columns),
        grad_down[:, :rank_cols],
        grad_bq,
        grad_down[:, rank_cols:],
        grad_bv,
    )


LANES = 128
MESH = pl.DeviceIdType.MESH
NP = 4
WP = 2


def paired_kernel(
    hid_ref,
    wq_ref,
    wk_ref,
    wv_ref,
    aq_ref,
    av_ref,
    bq_ref,
    bv_ref,
    pos_ref,
    og_ref,
    out_ref,
    gaq_ref,
    gbq_ref,
    gav_ref,
    gbv_ref,
    hbuf,
    wbuf,
    relay,
    psend,
    precv,
    lsend,
    lrecv,
    qkv,
    lowt,
    ball,
    ogbuf,
    posbuf,
    ctab,
    stab,
    osend,
    orecv,
    gbs,
    gbr,
    lgacc,
    lgs,
    lgr,
    gas,
    gar,
    aqbuf,
    avbuf,
    bqbuf,
    bvbuf,
    second_sem,
    third_sem,
    local_sem,
    hz_send,
    hxr_send,
    rl_recv,
    hx_send,
    hs_send,
    h_recv,
    w_send,
    wy_send,
    w_recv,
    p_send,
    p_recv,
    l_send,
    l_recv,
    q_send,
    q_recv,
    lq_send,
    lq_recv,
    og_send,
    og_recv,
    pos_send,
    pos_recv,
    o_send,
    o_recv,
    gb_send,
    gb_recv,
    lg_send,
    lg_recv,
    ga_send,
    ga_recv,
):
    f32, bf16 = jnp.float32, jnp.bfloat16
    rows, width = hid_ref.shape
    depth = wq_ref.shape[0]
    hl = rows // 2
    pr = hl // NP
    wrows = depth // (2 * WP)
    chunks = 2 * 4
    slice_k = 2 * width // 4
    r, c = lax.axis_index("rep"), lax.axis_index("ctx")
    h, s = lax.axis_index("head"), lax.axis_index("sub")
    m = c // 2
    inner = (c == 1) | (c == 2)
    outer = (c == 0) | (c == 3)
    near = 1 + m
    far_c = 3 - c
    rim = 3 * m
    home = h == m
    away = h != m
    me = c * 4 + h * 2 + s
    weights = (wq_ref, wk_ref, wv_ref)
    dot_t = functools.partial(
        lax.dot_general, dimension_numbers=(((1,), (1,)), ((), ())), preferred_element_type=f32
    )
    t_dot = functools.partial(
        lax.dot_general, dimension_numbers=(((0,), (0,)), ((), ())), preferred_element_type=f32
    )

    def member(number):
        hs = lax.rem(number, 4)
        return {"ctx": number // 4, "head": hs // 2, "sub": lax.rem(hs, 2)}

    def remote(src, dst, send, recv, device):
        return pltpu.make_async_remote_copy(
            src_ref=src, dst_ref=dst, send_sem=send, recv_sem=recv, device_id=device, device_id_type=MESH
        )

    def rows_at(start, size):
        return pl.ds(pl.multiple_of(start, 16), size)

    def cols(number, size):
        return pl.ds(pl.multiple_of(number * size, LANES), size)

    barrier = pltpu.get_barrier_semaphore()

    def greet(semaphore):
        for cond, device in ((c > 0, {"ctx": c - 1}), (c < 3, {"ctx": c + 1})):

            @pl.when(cond)
            def _():
                pl.semaphore_signal(semaphore, inc=1, device_id=device, device_id_type=MESH)

    greet(barrier)
    for axis, place in (("head", h), ("sub", s), ("rep", r)):
        pl.semaphore_signal(barrier, inc=1, device_id={axis: 1 - place}, device_id_type=MESH)

    def own_piece(e, p):
        return hid_ref.at[pl.ds(e * hl + p * pr, pr), :]

    def chunk_of(b, e, hd):
        return lax.rem(2 * b + e - hd + chunks, chunks)

    def hslot(b, e, p, hd, q):
        return hbuf.at[rows_at(chunk_of(b, e, hd) * hl + p * pr, pr), cols(q, width)]

    def wslot(j, t, quarter, side, w):
        return wbuf.at[j, t, rows_at(quarter * depth + side * (depth // 2) + w * wrows, wrows), :]

    own_h = [
        pltpu.make_async_copy(
            hid_ref.at[pl.ds(e * hl, hl), :],
            hbuf.at[rows_at(chunk_of(c, e, h) * hl, hl), cols(s, width)],
            local_sem.at[e],
        )
        for e in range(2)
    ]
    own_pos = pltpu.make_async_copy(pos_ref, posbuf.at[c], local_sem.at[2])
    own_og = [
        pltpu.make_async_copy(og_ref.at[pl.ds(0, hl), :], ogbuf.at[pl.ds(0, hl), :], local_sem.at[3]),
        pltpu.make_async_copy(
            og_ref.at[pl.ds(hl, hl), :], ogbuf.at[rows_at(hl - h * hl, hl), :], local_sem.at[4]
        ),
    ]

    def own_w(j, t):
        return pltpu.make_async_copy(
            weights[t].at[:, pl.ds(j * LANES, LANES)],
            wbuf.at[j, t, rows_at((c - 2 * m) * depth, depth), :],
            local_sem.at[5 + 3 * j + t],
        )

    factors = [
        pltpu.make_async_copy(src, dst, local_sem.at[17 + k])
        for k, (src, dst) in enumerate(
            ((aq_ref, aqbuf), (av_ref, avbuf), (bq_ref, bqbuf), (bv_ref, bvbuf))
        )
    ]
    for copy in factors:
        copy.start()
    own_pos.start()

    @pl.when(inner & home)
    def _():
        for copy in own_h:
            copy.start()

    @pl.when(inner)
    def _():
        for j in range(4):
            for t in range(3):
                own_w(j, t).start()

    own_og[1].start()
    pl.when(h == 0)(own_og[0].start)
    beside = jnp.where(inner, 2, 1)
    pl.semaphore_wait(barrier, 3 + beside)
    greet(second_sem)

    def h_direct(p):
        return remote(own_piece(1, p), hslot(c, 1, p, h, s), hz_send.at[0, p], h_recv.at[c, 1, p, s], {"ctx": 1 + h})

    def h_relay_in(p):
        return remote(
            own_piece(0, p), relay.at[pl.ds(p * pr, pr), :], hxr_send.at[p], rl_recv.at[p], {"head": 1 - h}
        )

    def h_relay_out(p):
        return remote(
            relay.at[pl.ds(p * pr, pr), :],
            hslot(c, 0, p, h, s),
            hz_send.at[1, p],
            h_recv.at[c, 0, p, s],
            {"ctx": 2 - h},
        )

    direct_on = c != 1 + h
    relay_on = c != 2 - h

    def h_cross(b, e, p, src=None):
        return remote(
            hslot(b, e, p, h, s) if src is None else src,
            hslot(b, e, p, 1 - h, s),
            hx_send.at[b, e, p],
            h_recv.at[b, e, p, s],
            {"head": 1 - h},
        )

    def h_twin(b, e, p, src=None):
        land = hslot(b, e, p, h, s)
        return remote(
            land if src is None else src, land, hs_send.at[b, e, p], h_recv.at[b, e, p, s], {"sub": 1 - s}
        )

    def h_arrived(b, e, p, q):
        land = hslot(b, e, p, h, q)
        return remote(land, land, hx_send.at[0, 0, 0], h_recv.at[b, e, p, q], {"sub": 1 - s})

    def w_out(j, t, w):
        return remote(
            weights[t].at[rows_at(r * (depth // 2) + w * wrows, wrows), pl.ds(j * LANES, LANES)],
            wslot(j, t, c - 2 * m, r, w),
            w_send.at[j, t, w],
            w_recv.at[j, t, r, w],
            {"ctx": near},
        )

    other = 1 - (c - 2 * m)

    def w_pass(j, t, w):
        land = wslot(j, t, other, r, w)
        return remote(land, land, wy_send.at[j, t, w], w_recv.at[j, t, r, w], {"rep": 1 - r})

    def w_arrived(j, t, w):
        land = wslot(j, t, other, 1 - r, w)
        return remote(land, land, wy_send.at[0, 0, 0], w_recv.at[j, t, 1 - r, w], {"rep": 1 - r})

    def half_of(g, side):
        return rows_at(jnp.where(g == 0, 1 - side, side) * rows, rows)

    def p_out(j, t, g, side=None):
        here = half_of(g, 1 - m if side is None else side)
        return remote(
            psend.at[j, t, here], precv.at[j, t, here], p_send.at[j, t, g], p_recv.at[j, t, g], {"ctx": 3 - c}
        )

    def l_out(g):
        return remote(lsend.at[g], lrecv.at[g], l_send.at[g], l_recv.at[g], {"ctx": 3 - c})

    def q_out(j, t):
        land = qkv.at[j, t, rows_at(m * rows, rows)]
        return remote(land, land, q_send.at[j, t], q_recv.at[j, t], {"ctx": rim})

    lq_out = remote(lowt.at[m], lowt.at[m], lq_send.at[0], lq_recv.at[0], {"ctx": rim})
    og_out = remote(
        og_ref.at[pl.ds(0, hl), :], ogbuf.at[pl.ds(hl, hl), :], og_send.at[0], og_recv.at[0], {"ctx": lax.rem(c + 3, 4)}
    )

    def pos_out(k):
        return remote(pos_ref, posbuf.at[c], pos_send.at[k - 1], pos_recv.at[c], {"ctx": lax.rem(c + k, 4)})

    def o_out(j):
        return remote(osend.at[j], orecv.at[j], o_send.at[j], o_recv.at[j], {"ctx": lax.rem(c + 1, 4)})

    def gb_out(j, k):
        return remote(gbs.at[j], gbr.at[c, j], gb_send.at[j, k - 1], gb_recv.at[j, c], {"ctx": lax.rem(c + k, 4)})

    def tables():
        for block in range(4):

            @pl.when(block != c)
            def _():
                remote(pos_ref, posbuf.at[block], pos_send.at[0], pos_recv.at[block], {"sub": 1 - s}).wait_recv()

        own_pos.wait()
        lane = lax.broadcasted_iota(jnp.int32, (LANES, LANES), 1)
        half_dim = LANES // 2
        index = lax.broadcasted_iota(jnp.int32, (8, LANES), 1) % half_dim
        inverse = jnp.exp(index.astype(f32) * (-2.0 * math.log(10000.0) / HEAD_DIM))[0:1, :]

        def one(number, carry):
            place = lax.rem(4 * m + number + h, chunks)
            row = posbuf[place // 2, pl.ds(lax.rem(place, 2), 1), :].astype(f32)
            column = jnp.transpose(jnp.broadcast_to(row, (LANES, LANES)))
            angle = (column * (TRAIN_CTX / MAX_POS)) * inverse
            here = pl.ds(pl.multiple_of(number * LANES, LANES), LANES)
            ctab[here, :] = jnp.cos(angle)
            sine = jnp.sin(angle)
            stab[here, :] = jnp.where(lane < LANES // 2, -sine, sine)
            return carry

        lax.fori_loop(0, 4, one, 0)

    def turn(u, cosine, sine):
        return u * cosine + pltpu.roll(u, LANES // 2, 1) * sine

    scale = 1.0 / math.sqrt(HEAD_DIM)
    mine = rows_at((c - 2 * m) * rows, rows)

    def attend(j):
        here = cols(j, LANES)
        q, k, v, grad = qkv[j, 0, mine], qkv[j, 1, mine], qkv[j, 2, mine], ogbuf[:, here]
        allowed = lax.broadcasted_iota(jnp.int32, (rows, rows), 0) >= lax.broadcasted_iota(
            jnp.int32, (rows, rows), 1
        )
        scores = jnp.where(allowed, dot_t(q, k) * scale, -jnp.inf)
        highest = jnp.max(scores, axis=-1, keepdims=True)
        expo = jnp.exp(scores - highest)
        probs = expo * (1.0 / jnp.sum(expo, axis=-1, keepdims=True))
        probs_b = probs.astype(bf16)
        out = jnp.dot(probs_b, v, preferred_element_type=f32).astype(bf16)
        osend[j] = out[hl:]

        @pl.when(h == 0)
        def _():
            out_ref[:, here] = out

        @pl.when(h == 1)
        def _():
            o_out(j).start()
            out_ref[pl.ds(hl, hl), here] = out[:hl]

        dprob = dot_t(grad, v)
        delta = jnp.sum(grad.astype(f32) * out.astype(f32), axis=-1, keepdims=True)
        dscore_b = (probs * (dprob - delta) * scale).astype(bf16)
        dq = jnp.dot(dscore_b, k, preferred_element_type=f32)
        dq = turn(dq, ctab[mine, :], -stab[mine, :]).astype(bf16)
        dv = t_dot(probs_b, grad).astype(bf16)
        lgacc[...] += 2.0 * (dot_t(ball[0, :, here], dq) + dot_t(ball[2, :, here], dv))
        low = lowt[c - 2 * m]
        gbs[j, 0:8, :] = (2.0 * jnp.dot(low, dq, preferred_element_type=f32))[0:8]
        gbs[j, 8:16, :] = (2.0 * jnp.dot(low, dv, preferred_element_type=f32))[8:16]
        for k_ in range(1, 4):
            gb_out(j, k_).start()

    def reach():
        pl.semaphore_wait(second_sem, beside)
        greet(third_sem)
        pl.semaphore_wait(third_sem, beside)
        for k in range(1, 4):
            pos_out(k).start()

    def factors_in():
        for copy in factors:
            copy.wait()
        nothing = jnp.zeros((8, 4 * LANES), f32)
        ball[0] = jnp.concatenate([bqbuf[...].astype(f32), nothing], axis=0).astype(bf16)
        ball[1] = jnp.concatenate([nothing, nothing], axis=0).astype(bf16)
        ball[2] = jnp.concatenate([nothing, bvbuf[...].astype(f32)], axis=0).astype(bf16)
        lgacc[...] = jnp.zeros(lgacc.shape, f32)

    def og_in():
        @pl.when(h == 1)
        def _():
            og_out.wait_recv()
            own_og[1].wait()

        @pl.when(h == 0)
        def _():
            own_og[0].wait()
            own_og[1].wait()

    @pl.when(inner)
    def _():
        e = jnp.where(home, 1, 0)

        @pl.when(home)
        def _():
            for half in range(2):
                for p in range(NP):
                    h_twin(c, half, p, own_piece(half, p)).start()

        @pl.when(away)
        def _():
            for p in range(NP):
                h_relay_in(p).start()
                h_direct(p).start()

        def z_in(b, p):
            h_arrived(b, e, p, s).wait_recv()
            h_cross(b, e, p).start()
            h_twin(b, e, p).start()

        def x_in(b, half, p):
            h_arrived(b, half, p, s).wait_recv()
            h_twin(b, half, p).start()

        def twin_in(b):
            for half in range(2):
                for p in range(NP):
                    h_arrived(b, half, p, 1 - s).wait_recv()

        def forward(j, t):
            for w in range(WP):
                copy = w_pass(j, t, w)
                copy.wait_recv()
                copy.start()

        def passed(j, t):
            for w in range(WP):
                w_arrived(j, t, w).wait_recv()

        def group_rows(g):
            return rows_at(g * rows, rows)

        def side_rows(side):
            return rows_at(side * 2 * rows, 2 * rows)

        def partner(j, t, g):
            here = half_of(g, 1 - m)
            group = jnp.where(g == 0, 3 - c, 3 * (1 - m))
            y = jnp.dot(hbuf[group_rows(group), :], wbuf[j, t], preferred_element_type=f32)
            psend[j, t, here] = y.astype(bf16)
            p_out(j, t, g).start()

        def partner_both(j, t):
            y = jnp.dot(hbuf[side_rows(1 - m), :], wbuf[j, t], preferred_element_type=f32)
            psend[j, t] = y.astype(bf16)
            p_out(j, t, 1).start()
            p_out(j, t, 0).start()

        whole = [(half, p) for half in range(2) for p in range(NP)]
        pieces = [(t, w) for t in range(3) for w in range(WP)]
        rest = list(pieces)

        def forward_piece(j, t, w):
            copy = w_pass(j, t, w)
            copy.wait_recv()
            copy.start()

        reach()
        for p in range(NP):

            @pl.when(home)
            def _():
                h_relay_in(p).wait_recv()
                h_relay_out(p).start()

            z_in(3 - c, p)
            forward_piece(0, *rest.pop(0))
        factors_in()
        tables()

        @pl.when(home)
        def _():
            for half, p in whole[:2]:
                h_cross(c, half, p, own_piece(half, p)).start()

        while rest:
            forward_piece(0, *rest.pop(0))
        pl.when(h == 1)(og_out.start)
        far = 3 * (1 - m)
        late = (c == 1) & (h == 1)

        def first_in(t, carry):
            partner(0, t, 0)
            return carry

        def first_out(t, carry):
            partner(0, t, 1)
            return carry

        for p in range(NP // 2):
            z_in(far, p)
        for p in range(NP):
            x_in(3 - c, 1 - e, p)
            if p + NP // 2 < NP - 1:
                z_in(far, p + NP // 2)
        twin_in(3 - c)

        @pl.when(home)
        def _():
            for copy in own_h:
                copy.wait()
            twin_in(c)

        for t in range(3):
            own_w(0, t).wait()
            passed(0, t)

        @pl.when(jnp.logical_not(late))
        def _():
            lax.fori_loop(0, 3, first_in, 0)

        z_in(far, NP - 1)
        for p in range(NP):
            z_in(rim, p)
            x_in(far, 1 - e, p)

        @pl.when(home)
        def _():
            for half, p in whole[2:]:
                h_cross(c, half, p, own_piece(half, p)).start()

        twin_in(far)

        @pl.when(late)
        def _():
            lax.fori_loop(0, 3, first_in, 0)

        forward(1, 0)
        for p in range(NP):
            x_in(rim, 1 - e, p)
        twin_in(rim)
        lax.fori_loop(0, 3, first_out, 0)
        for j in range(1, 4):
            for t in range(3):
                own_w(j, t).wait()
        a_both = jnp.concatenate(
            [
                aqbuf[:, pl.ds(pl.multiple_of(m * 2 * width, LANES), 2 * width)].astype(f32),
                avbuf[:, pl.ds(pl.multiple_of(m * 2 * width, LANES), 2 * width)].astype(f32),
            ],
            axis=0,
        ).astype(bf16)

        def low_other(g, carry):
            group = 2 * (1 - m) + g
            lsend[g] = dot_t(a_both, hbuf[group_rows(group), :])
            l_out(g).start()
            return carry

        forward(1, 1)
        lax.fori_loop(0, 2, low_other, 0)

        def low_own(g, carry):
            group = 2 * m + g
            l_out(g).wait_recv()
            lowt[g] = (dot_t(a_both, hbuf[group_rows(group), :]) + lrecv[g]).astype(bf16)
            return carry

        def finish(i):
            j, t = i // 3, lax.rem(i, 3)
            plain = t == 2

            low = jnp.concatenate([lowt[0], lowt[1]], axis=1)
            y = jnp.dot(hbuf[side_rows(m), :], wbuf[j, t], preferred_element_type=f32)
            y = y + 2.0 * t_dot(low, ball[t, :, cols(j, LANES)])
            cosine = jnp.where(plain, 1.0, ctab[...])
            sine = jnp.where(plain, 0.0, stab[...])
            for g in (1, 0):
                p_out(j, t, g, m).wait_recv()
            qkv[j, t] = turn(y + precv[j, t].astype(f32), cosine, sine).astype(bf16)
            q_out(j, t).start()

        def slot(i, carry):
            @pl.when(i < 13)
            def _():
                j, t = (i - 1) // 3, lax.rem(i - 1, 3)
                passed(j, t)

                partner_both(j, t)

            @pl.when(i < 11)
            def _():
                forward((i + 1) // 3, lax.rem(i + 1, 3))

            @pl.when(i == 6)
            def _():
                @pl.when(away)
                def _():
                    for half, p in whole:
                        x_in(c, half, p)
                    twin_in(c)

                lax.fori_loop(0, 2, low_own, 0)
                lq_out.start()

            first = jnp.where(i == 6, 0, jnp.where(i == 7, 2, i - 4))
            count = jnp.where(i < 6, 0, jnp.where(i < 8, 2, 1))

            def some(k, carry_):
                finish(first + k)
                return carry_

            lax.fori_loop(0, count, some, 0)

            pl.when(i == 7)(og_in)

            @pl.when((i == 7) | (i == 9) | (i == 12) | (i == 15))
            def _():
                attend(jnp.where(i == 15, 3, (i - 6) // 2 - jnp.where(i == 12, 1, 0)))

            return carry

        lax.fori_loop(4, 16, slot, 0)

    @pl.when(outer)
    def _():
        for t in range(3):
            for w in range(WP):
                w_out(0, t, w).start()
        for p in range(NP):
            h_relay_in(p).start()
        reach()

        def relays():
            for p in range(NP):
                h_relay_in(p).wait_recv()
                h_relay_out(p).start()

        @pl.when(home)
        def _():
            relays()
            for p in range(NP):
                h_direct(p).start()

        @pl.when(away)
        def _():
            for p in range(NP):
                h_direct(p).start()
            relays()

        def send_w(j, carry):
            for t in range(3):
                for w in range(WP):
                    remote(
                        weights[t].at[rows_at(r * (depth // 2) + w * wrows, wrows), cols(j, LANES)],
                        wslot(j, t, c - 2 * m, r, w),
                        w_send.at[j, t, w],
                        w_recv.at[j, t, r, w],
                        {"ctx": near},
                    ).start()
            return carry

        send_w(1, 0)
        pl.when(h == 1)(og_out.start)
        lax.fori_loop(2, 4, send_w, 0)
        factors_in()
        tables()
        og_in()
        remote(lowt.at[m], lowt.at[m], lq_send.at[0], lq_recv.at[0], {"sub": 1 - s}).wait_recv()

        def one(j, carry):
            for t in range(3):
                q_out(j, t).wait_recv()
            attend(j)
            return carry

        lax.fori_loop(0, 4, one, 0)

    lgs[...] = lgacc[...].astype(bf16)
    lgr[me] = lgs[...]

    def lg_out(k):
        dest = 4 + k
        return remote(lgs, lgr.at[me], lg_send.at[k], lg_recv.at[me], member(dest))

    for k in range(8):
        pl.when(me != 4 + k)(lg_out(k).start)

    for p in range(NP):
        pl.when(direct_on)(h_direct(p).wait_send)
        pl.when(direct_on)(h_relay_in(p).wait_send)
        pl.when(relay_on)(h_relay_out(p).wait_send)
    for k in range(1, 4):
        pos_out(k).wait_send()
    pl.when(h == 1)(og_out.wait_send)

    @pl.when(outer)
    def _():
        for j in range(4):
            for t in range(3):
                for w in range(WP):
                    w_out(j, t, w).wait_send()

    @pl.when(inner)
    def _():
        for b in range(4):
            for half in range(2):
                for p in range(NP):
                    h_twin(b, half, p).wait_send()
                    crossed = ((b == c) & home) | ((b != c) & (home == (half == 1)))
                    pl.when(crossed)(h_cross(b, half, p).wait_send)
        for j in range(4):
            for t in range(3):
                for w in range(WP):
                    w_pass(j, t, w).wait_send()
                for g in range(2):
                    p_out(j, t, g).wait_send()
                q_out(j, t).wait_send()
        for g in range(2):
            l_out(g).wait_send()
        lq_out.wait_send()

    def ga_out(k):
        dest = lax.rem(me + k, 16)
        return remote(gas, gar.at[me - 4], ga_send.at[k - 1], ga_recv.at[me - 4], member(dest))

    @pl.when(inner)
    def _():
        for k in range(1, 16):
            frm = lax.rem(me + k, 16)
            remote(lgs, lgr.at[frm], lg_send.at[0], lg_recv.at[frm], {"sub": 1 - s}).wait_recv()

        def side(hd):
            return jnp.concatenate(
                [
                    lgr[4 * g + 2 * hd].astype(f32) + lgr[4 * g + 2 * hd + 1].astype(f32)
                    for g in range(4)
                ],
                axis=1,
            )

        zero, one = side(0), side(1)
        wide_ = 4 * rows
        right = jnp.concatenate([one[:, wide_ - hl :], one[:, : wide_ - hl]], axis=1)
        left = jnp.concatenate([zero[:, hl:], zero[:, :hl]], axis=1)
        low = jnp.where(h == 0, zero + right, left + one)
        upper = low.astype(bf16)
        lower = (low - upper.astype(f32)).astype(bf16)
        both = jnp.concatenate([upper, lower], axis=0)
        part_ = jnp.dot(both, hbuf[:, cols(h * 2 + s, slice_k)], preferred_element_type=f32)
        gas[...] = (part_[0:16] + part_[16:32]).astype(bf16)
        gar[me - 4] = gas[...]
        for k in range(1, 16):
            ga_out(k).start()

    @pl.when(h == 1)
    def _():
        for j in range(4):
            o_out(j).wait_recv()
            out_ref[0:hl, j * LANES : (j + 1) * LANES] = orecv[j]

    for j in range(4):
        for block in range(4):

            @pl.when(block != c)
            def _():
                remote(gbs.at[0], gbr.at[block, j], gb_send.at[0, 0], gb_recv.at[j, block], {"sub": 1 - s}).wait_recv()

        gbr[c, j] = gbs[j]
        total = (gbr[0, j] + gbr[1, j]) + (gbr[2, j] + gbr[3, j])
        gbq_ref[:, j * LANES : (j + 1) * LANES] = total[0:8]
        gbv_ref[:, j * LANES : (j + 1) * LANES] = total[8:16]

    for k in range(8):

        @pl.when(me != 4 + k)
        def _():
            remote(gas, gar.at[k], ga_send.at[0], ga_recv.at[k], {"sub": 1 - s}).wait_recv()

        block = gar[k].astype(f32)
        gaq_ref[:, k * slice_k : (k + 1) * slice_k] = block[0:8]
        gav_ref[:, k * slice_k : (k + 1) * slice_k] = block[8:16]

    @pl.when(h == 1)
    def _():
        for j in range(4):
            o_out(j).wait_send()

    for j in range(4):
        for k in range(1, 4):
            gb_out(j, k).wait_send()
    for k in range(8):
        pl.when(me != 4 + k)(lg_out(k).wait_send)

    @pl.when(inner)
    def _():
        for k in range(1, 16):
            ga_out(k).wait_send()


def hand_over_kernel(count, *refs):
    sources, results, stages, sems = refs[:count], refs[count : 2 * count], refs[2 * count : 3 * count], refs[-1]
    fetched = [pltpu.make_async_copy(sources[k], stages[k], sems.at[0, k]) for k in range(count)]
    stored = [pltpu.make_async_copy(stages[k], results[k], sems.at[1, k]) for k in range(count)]
    for copy in fetched:
        copy.start()
    for k in reversed(range(count)):
        fetched[k].wait()
        stored[k].start()
    for copy in stored:
        copy.wait()


def hand_over(*arrays):
    spec = pl.BlockSpec(memory_space=pl.ANY)
    count = len(arrays)
    return pl.pallas_call(
        functools.partial(hand_over_kernel, count),
        out_shape=tuple(jax.ShapeDtypeStruct(a.shape, a.dtype) for a in arrays),
        in_specs=[spec] * count,
        out_specs=[spec] * count,
        scratch_shapes=[pltpu.VMEM(a.shape, a.dtype) for a in arrays] + [pltpu.SemaphoreType.DMA((2, count))],
    )(*arrays)


def paired(
    hidden_states, w_query, w_key, w_value, a_query, a_value, b_query, b_value, positions, out_grad
):
    f32, bf16 = jnp.float32, jnp.bfloat16
    rows, width = hidden_states.shape
    model, rank = a_query.shape
    depth, columns = w_query.shape
    pos = positions.reshape(rows // LANES, LANES)
    vmem, dma = pltpu.VMEM, pltpu.SemaphoreType.DMA
    hbm_spec = pl.BlockSpec(memory_space=pl.ANY)
    vmem_spec = pl.BlockSpec(memory_space=pltpu.VMEM)
    out, gaq, gbq, gav, gbv = pl.pallas_call(
        paired_kernel,
        out_shape=(
            jax.ShapeDtypeStruct((rows, columns), bf16),
            jax.ShapeDtypeStruct((rank, model), f32),
            jax.ShapeDtypeStruct((rank, columns), f32),
            jax.ShapeDtypeStruct((rank, model), f32),
            jax.ShapeDtypeStruct((rank, columns), f32),
        ),
        in_specs=[hbm_spec] * 10,
        out_specs=[vmem_spec] * 5,
        scratch_shapes=[
            vmem((4 * rows, 2 * width), bf16),
            vmem((4, 3, 2 * depth, LANES), bf16),
            vmem((rows // 2, width), bf16),
            vmem((4, 3, 2 * rows, LANES), bf16),
            vmem((4, 3, 2 * rows, LANES), bf16),
            vmem((2, 16, rows), f32),
            vmem((2, 16, rows), f32),
            vmem((4, 3, 2 * rows, LANES), bf16),
            vmem((2, 16, rows), bf16),
            vmem((3, 16, columns), bf16),
            vmem((rows, columns), bf16),
            vmem((4, rows // LANES, LANES), jnp.int32),
            vmem((2 * rows, LANES), f32),
            vmem((2 * rows, LANES), f32),
            vmem((4, rows // 2, LANES), bf16),
            vmem((4, rows // 2, LANES), bf16),
            vmem((4, 16, LANES), f32),
            vmem((4, 4, 16, LANES), f32),
            vmem((16, rows), f32),
            vmem((16, rows), bf16),
            vmem((16, 16, rows), bf16),
            vmem((16, model // 8), bf16),
            vmem((8, 16, model // 8), bf16),
            vmem((rank, model), bf16),
            vmem((rank, model), bf16),
            vmem((rank, columns), bf16),
            vmem((rank, columns), bf16),
            pltpu.SemaphoreType.REGULAR,
            pltpu.SemaphoreType.REGULAR,
            dma((21,)),
            dma((2, NP)),
            dma((NP,)),
            dma((NP,)),
            dma((4, 2, NP)),
            dma((4, 2, NP)),
            dma((4, 2, NP, 2)),
            dma((4, 3, WP)),
            dma((4, 3, WP)),
            dma((4, 3, 2, WP)),
            dma((4, 3, 2)),
            dma((4, 3, 2)),
            dma((2,)),
            dma((2,)),
            dma((4, 3)),
            dma((4, 3)),
            dma((1,)),
            dma((1,)),
            dma((1,)),
            dma((1,)),
            dma((3,)),
            dma((4,)),
            dma((4,)),
            dma((4,)),
            dma((4, 3)),
            dma((4, 4)),
            dma((8,)),
            dma((16,)),
            dma((15,)),
            dma((8,)),
        ],
        compiler_params=pltpu.CompilerParams(
            collective_id=1, has_side_effects=True, vmem_limit_bytes=56 * 1024 * 1024
        ),
    )(
        hidden_states, w_query, w_key, w_value, a_query.T, a_value.T, b_query, b_value, pos, out_grad
    )
    out, gaq, gbq, gav, gbv = hand_over(out, gaq, gbq, gav, gbv)
    return (out, gaq.T, gbq, gav.T, gbv)


def fits_paired(mesh, args):
    hidden_states, w_query, a_query = args[0], args[1], args[4]
    return (
        mesh.shape["rep"] == 2
        and mesh.shape["ctx"] == 4
        and mesh.shape["head"] == 2
        and mesh.shape["sub"] == 2
        and w_query.shape[1] == 4 * HEAD_DIM
        and HEAD_DIM == LANES
        and HEADS == 16
        and a_query.shape[1] == 8
        and hidden_states.shape[0] == 2 * LANES
        and hidden_states.shape[1] == w_query.shape[0]
        and a_query.shape[0] == 4 * w_query.shape[0]
        and w_query.shape[0] == 1024
    )


def choose(mesh, *args):
    return paired(*args) if fits_paired(mesh, args) else local(*args)


def solution(mesh):
    in_specs = (
        P(("rep", "ctx"), ("head", "sub")),
        P("ctx", ("head", "sub")),
        P("ctx", ("head", "sub")),
        P("ctx", ("head", "sub")),
        P(),
        P(),
        P(None, ("head", "sub")),
        P(None, ("head", "sub")),
        P(("rep", "ctx")),
        P(("rep", "ctx"), ("head", "sub")),
    )
    out_specs = (
        P(("rep", "ctx"), ("head", "sub")),
        P(None, "rep"),
        P("rep", ("head", "sub")),
        P(None, "rep"),
        P("rep", ("head", "sub")),
    )
    return jax.shard_map(
        functools.partial(choose, mesh), mesh=mesh, in_specs=in_specs, out_specs=out_specs, check_vma=False
    )
```

```python
import functools
import math

import jax
import jax.numpy as jnp
from jax import lax
from jax.experimental import pallas as pl
from jax.experimental.pallas import tpu as pltpu
from jax.sharding import PartitionSpec as P

HEAD_DIM = 128
HEADS = 16
TRAIN_CTX = 4096
MAX_POS = 100000


def passed_along(block, axis, distance):
    devices = range(lax.axis_size(axis))
    route = [((i - distance) % len(devices), i) for i in devices]
    return lax.ppermute(block, axis, route)


def rope_tables(positions):
    half_dim = HEAD_DIM // 2
    inverse = jnp.exp(
        jnp.arange(half_dim, dtype=jnp.float32) * (-2.0 * math.log(10000.0) / HEAD_DIM)
    )
    scaled = positions.astype(jnp.float32) * (TRAIN_CTX / MAX_POS)
    angle = scaled[:, None] * inverse[None, :]
    return (jnp.cos(angle)[:, None, :], jnp.sin(angle)[:, None, :])


def rotate(vectors, cosine, sine):
    half_dim = vectors.shape[-1] // 2
    first = vectors[..., :half_dim]
    second = vectors[..., half_dim:]
    return jnp.concatenate(
        [first * cosine - second * sine, second * cosine + first * sine], axis=-1
    )


def project_back(features, low_grads):
    block_width = min(features.shape[1], 512)
    block_count = features.shape[1] // block_width

    def one_block(number):
        section = lax.dynamic_slice_in_dim(features, number * block_width, block_width, 1).astype(
            jnp.float32
        )
        return lax.dot_general(
            section, low_grads, (((0,), (0,)), ((), ())), precision=lax.Precision.HIGHEST
        )

    blocks = lax.map(one_block, jnp.arange(block_count))
    return blocks.reshape(features.shape[1], low_grads.shape[1])


def local(
    hidden_states, w_query, w_key, w_value, a_query, a_value, b_query, b_value, positions, out_grad
):
    rows_here = hidden_states.shape[0]
    columns = w_query.shape[1]
    heads_here = columns // HEAD_DIM
    rank_cols = a_query.shape[1]
    scale = 1.0 / math.sqrt(HEAD_DIM)
    shard_count = lax.axis_size("ctx")
    total_tokens = rows_here * shard_count
    group_len = total_tokens // 4
    reach = (group_len // 2 % rows_here + group_len - 1) // rows_here
    full_states = lax.all_gather(hidden_states, ("head", "sub"), axis=1, tiled=True)
    pieces = (
        lax.all_gather(w_query, "ctx", axis=0, tiled=True),
        lax.all_gather(w_key, "ctx", axis=0, tiled=True),
        lax.all_gather(w_value, "ctx", axis=0, tiled=True),
    )
    base_q, base_k, base_v = tuple(
        (
            jnp.dot(full_states, weights_piece, preferred_element_type=jnp.float32)
            for weights_piece in pieces
        )
    )
    low_q = jnp.dot(full_states, a_query, preferred_element_type=jnp.float32).astype(jnp.bfloat16)
    low_v = jnp.dot(full_states, a_value, preferred_element_type=jnp.float32).astype(jnp.bfloat16)
    cosine, sine = rope_tables(positions)
    pre_q = base_q + 2.0 * jnp.dot(low_q, b_query, preferred_element_type=jnp.float32)
    queries = rotate(pre_q.reshape(rows_here, heads_here, HEAD_DIM), cosine, sine).astype(
        jnp.bfloat16
    )
    keyed = rotate(base_k.reshape(rows_here, heads_here, HEAD_DIM), cosine, sine).astype(
        jnp.bfloat16
    )
    valued = (base_v + 2.0 * jnp.dot(low_v, b_value, preferred_element_type=jnp.float32)).astype(
        jnp.bfloat16
    )
    valued = valued.reshape(rows_here, heads_here, HEAD_DIM)
    current = jnp.stack([keyed, valued])
    collected = [current]
    for level in range(reach):
        current = passed_along(current, "ctx", 1)
        collected.append(current)
    key_rows = jnp.concatenate([block[0] for block in collected], axis=0)
    value_rows = jnp.concatenate([block[1] for block in collected], axis=0)
    shard_id = lax.axis_index("ctx")
    head_ids = lax.axis_index(("head", "sub")) * heads_here + jnp.arange(heads_here)
    amount = jnp.where(head_ids >= HEADS // 2, group_len // 2, 0).astype(jnp.int32)
    query_pos = shard_id * rows_here + jnp.arange(rows_here, dtype=jnp.int32)
    block_ids = jnp.arange(reach + 1, dtype=jnp.int32)
    source_shard = (shard_id - block_ids) % shard_count
    key_pos = (
        source_shard[:, None] * rows_here + jnp.arange(rows_here, dtype=jnp.int32)[None, :]
    ).reshape(-1)
    query_num = (query_pos[None, :] - amount[:, None]) % total_tokens
    key_num = (key_pos[None, :] - amount[:, None]) % total_tokens
    same_group = key_num[:, None, :] // group_len == query_num[:, :, None] // group_len
    visible = same_group & (key_num[:, None, :] <= query_num[:, :, None])
    scores = (
        jnp.einsum("qhd,khd->hqk", queries, key_rows, preferred_element_type=jnp.float32) * scale
    )
    scores = jnp.where(visible, scores, -jnp.inf)
    highest = jnp.max(scores, axis=-1, keepdims=True)
    expo = jnp.where(visible, jnp.exp(scores - highest), 0.0)
    probs = expo / jnp.sum(expo, axis=-1, keepdims=True)
    probs_b = probs.astype(jnp.bfloat16)
    attended = jnp.einsum("hqk,khd->qhd", probs_b, value_rows, preferred_element_type=jnp.float32)
    attn_out = attended.astype(jnp.bfloat16)
    grads = out_grad.reshape(rows_here, heads_here, HEAD_DIM)
    dprob = jnp.einsum("qhd,khd->hqk", grads, value_rows, preferred_element_type=jnp.float32)
    delta = jnp.sum(grads.astype(jnp.float32) * attn_out.astype(jnp.float32), axis=-1)
    dscore = probs * (dprob - delta.T[:, :, None])
    dscore_b = (dscore * scale).astype(jnp.bfloat16)
    dquery = jnp.einsum("hqk,khd->qhd", dscore_b, key_rows, preferred_element_type=jnp.float32)
    dvalue = jnp.einsum("hqk,qhd->khd", probs_b, grads, preferred_element_type=jnp.float32)
    value_blocks = dvalue.reshape(reach + 1, rows_here, columns)
    carried = value_blocks[reach]
    for level in range(reach, 0, -1):
        carried = passed_along(carried, "ctx", -1) + value_blocks[level - 1]
    dv_local = carried.astype(jnp.bfloat16)
    dq_local = rotate(dquery, cosine, -sine).astype(jnp.bfloat16).reshape(rows_here, columns)
    grad_bq = 2.0 * jnp.dot(low_q.T, dq_local, preferred_element_type=jnp.float32)
    grad_bv = 2.0 * jnp.dot(low_v.T, dv_local, preferred_element_type=jnp.float32)
    low_grads = jnp.concatenate(
        [
            2.0 * jnp.dot(dq_local, b_query.T, preferred_element_type=jnp.float32),
            2.0 * jnp.dot(dv_local, b_value.T, preferred_element_type=jnp.float32),
        ],
        axis=1,
    )
    grad_down = lax.psum(project_back(full_states, low_grads), ("ctx", "head", "sub"))
    grad_bq, grad_bv = lax.psum((grad_bq, grad_bv), "ctx")
    return (
        attn_out.reshape(rows_here, columns),
        grad_down[:, :rank_cols],
        grad_bq,
        grad_down[:, rank_cols:],
        grad_bv,
    )


LANES = 128
MESH = pl.DeviceIdType.MESH
NP = 4
WP = 2


def paired_kernel(
    hid_ref,
    wq_ref,
    wk_ref,
    wv_ref,
    aq_ref,
    av_ref,
    bq_ref,
    bv_ref,
    pos_ref,
    og_ref,
    out_ref,
    gaq_ref,
    gbq_ref,
    gav_ref,
    gbv_ref,
    hbuf,
    wbuf,
    relay,
    psend,
    precv,
    lsend,
    lrecv,
    qkv,
    lowt,
    ball,
    ogbuf,
    posbuf,
    ctab,
    stab,
    osend,
    orecv,
    gbs,
    gbr,
    lgacc,
    lgs,
    lgr,
    gas,
    gar,
    aqbuf,
    avbuf,
    bqbuf,
    bvbuf,
    second_sem,
    third_sem,
    local_sem,
    hz_send,
    hxr_send,
    rl_recv,
    hx_send,
    hs_send,
    h_recv,
    w_send,
    wy_send,
    w_recv,
    p_send,
    p_recv,
    l_send,
    l_recv,
    q_send,
    q_recv,
    lq_send,
    lq_recv,
    og_send,
    og_recv,
    pos_send,
    pos_recv,
    o_send,
    o_recv,
    gb_send,
    gb_recv,
    lg_send,
    lg_recv,
    ga_send,
    ga_recv,
):
    f32, bf16 = jnp.float32, jnp.bfloat16
    rows, width = hid_ref.shape
    depth = wq_ref.shape[0]
    hl = rows // 2
    pr = hl // NP
    wrows = depth // (2 * WP)
    chunks = 2 * 4
    slice_k = 2 * width // 4
    r, c = lax.axis_index("rep"), lax.axis_index("ctx")
    h, s = lax.axis_index("head"), lax.axis_index("sub")
    m = c // 2
    inner = (c == 1) | (c == 2)
    outer = (c == 0) | (c == 3)
    near = 1 + m
    far_c = 3 - c
    rim = 3 * m
    home = h == m
    away = h != m
    me = c * 4 + h * 2 + s
    weights = (wq_ref, wk_ref, wv_ref)
    dot_t = functools.partial(
        lax.dot_general, dimension_numbers=(((1,), (1,)), ((), ())), preferred_element_type=f32
    )
    t_dot = functools.partial(
        lax.dot_general, dimension_numbers=(((0,), (0,)), ((), ())), preferred_element_type=f32
    )

    def member(number):
        hs = lax.rem(number, 4)
        return {"ctx": number // 4, "head": hs // 2, "sub": lax.rem(hs, 2)}

    def remote(src, dst, send, recv, device):
        return pltpu.make_async_remote_copy(
            src_ref=src, dst_ref=dst, send_sem=send, recv_sem=recv, device_id=device, device_id_type=MESH
        )

    def rows_at(start, size):
        return pl.ds(pl.multiple_of(start, 16), size)

    def cols(number, size):
        return pl.ds(pl.multiple_of(number * size, LANES), size)

    barrier = pltpu.get_barrier_semaphore()

    def greet(semaphore):
        for cond, device in ((c > 0, {"ctx": c - 1}), (c < 3, {"ctx": c + 1})):

            @pl.when(cond)
            def _():
                pl.semaphore_signal(semaphore, inc=1, device_id=device, device_id_type=MESH)

    greet(barrier)
    for axis, place in (("head", h), ("sub", s), ("rep", r)):
        pl.semaphore_signal(barrier, inc=1, device_id={axis: 1 - place}, device_id_type=MESH)

    def own_piece(e, p):
        return hid_ref.at[pl.ds(e * hl + p * pr, pr), :]

    def chunk_of(b, e, hd):
        return lax.rem(2 * b + e - hd + chunks, chunks)

    def hslot(b, e, p, hd, q):
        return hbuf.at[rows_at(chunk_of(b, e, hd) * hl + p * pr, pr), cols(q, width)]

    def wslot(j, t, quarter, side, w):
        return wbuf.at[j, t, rows_at(quarter * depth + side * (depth // 2) + w * wrows, wrows), :]

    own_h = [
        pltpu.make_async_copy(
            hid_ref.at[pl.ds(e * hl, hl), :],
            hbuf.at[rows_at(chunk_of(c, e, h) * hl, hl), cols(s, width)],
            local_sem.at[e],
        )
        for e in range(2)
    ]
    own_pos = pltpu.make_async_copy(pos_ref, posbuf.at[c], local_sem.at[2])
    own_og = [
        pltpu.make_async_copy(og_ref.at[pl.ds(0, hl), :], ogbuf.at[pl.ds(0, hl), :], local_sem.at[3]),
        pltpu.make_async_copy(
            og_ref.at[pl.ds(hl, hl), :], ogbuf.at[rows_at(hl - h * hl, hl), :], local_sem.at[4]
        ),
    ]

    def own_w(j, t):
        return pltpu.make_async_copy(
            weights[t].at[:, pl.ds(j * LANES, LANES)],
            wbuf.at[j, t, rows_at((c - 2 * m) * depth, depth), :],
            local_sem.at[5 + 3 * j + t],
        )

    factors = [
        pltpu.make_async_copy(src, dst, local_sem.at[17 + k])
        for k, (src, dst) in enumerate(
            ((aq_ref, aqbuf), (av_ref, avbuf), (bq_ref, bqbuf), (bv_ref, bvbuf))
        )
    ]
    for copy in factors:
        copy.start()
    own_pos.start()

    @pl.when(inner & home)
    def _():
        for copy in own_h:
            copy.start()

    @pl.when(inner)
    def _():
        for j in range(4):
            for t in range(3):
                own_w(j, t).start()

    own_og[1].start()
    pl.when(h == 0)(own_og[0].start)
    beside = jnp.where(inner, 2, 1)
    pl.semaphore_wait(barrier, 3 + beside)
    greet(second_sem)

    def h_direct(p):
        return remote(own_piece(1, p), hslot(c, 1, p, h, s), hz_send.at[0, p], h_recv.at[c, 1, p, s], {"ctx": 1 + h})

    def h_relay_in(p):
        return remote(
            own_piece(0, p), relay.at[pl.ds(p * pr, pr), :], hxr_send.at[p], rl_recv.at[p], {"head": 1 - h}
        )

    def h_relay_out(p):
        return remote(
            relay.at[pl.ds(p * pr, pr), :],
            hslot(c, 0, p, h, s),
            hz_send.at[1, p],
            h_recv.at[c, 0, p, s],
            {"ctx": 2 - h},
        )

    direct_on = c != 1 + h
    relay_on = c != 2 - h

    def h_cross(b, e, p, src=None):
        return remote(
            hslot(b, e, p, h, s) if src is None else src,
            hslot(b, e, p, 1 - h, s),
            hx_send.at[b, e, p],
            h_recv.at[b, e, p, s],
            {"head": 1 - h},
        )

    def h_twin(b, e, p, src=None):
        land = hslot(b, e, p, h, s)
        return remote(
            land if src is None else src, land, hs_send.at[b, e, p], h_recv.at[b, e, p, s], {"sub": 1 - s}
        )

    def h_arrived(b, e, p, q):
        land = hslot(b, e, p, h, q)
        return remote(land, land, hx_send.at[0, 0, 0], h_recv.at[b, e, p, q], {"sub": 1 - s})

    def w_out(j, t, w):
        return remote(
            weights[t].at[rows_at(r * (depth // 2) + w * wrows, wrows), pl.ds(j * LANES, LANES)],
            wslot(j, t, c - 2 * m, r, w),
            w_send.at[j, t, w],
            w_recv.at[j, t, r, w],
            {"ctx": near},
        )

    other = 1 - (c - 2 * m)

    def w_pass(j, t, w):
        land = wslot(j, t, other, r, w)
        return remote(land, land, wy_send.at[j, t, w], w_recv.at[j, t, r, w], {"rep": 1 - r})

    def w_arrived(j, t, w):
        land = wslot(j, t, other, 1 - r, w)
        return remote(land, land, wy_send.at[0, 0, 0], w_recv.at[j, t, 1 - r, w], {"rep": 1 - r})

    def half_of(g, side):
        return rows_at(jnp.where(g == 0, 1 - side, side) * rows, rows)

    def p_out(j, t, g, side=None):
        here = half_of(g, 1 - m if side is None else side)
        return remote(
            psend.at[j, t, here], precv.at[j, t, here], p_send.at[j, t, g], p_recv.at[j, t, g], {"ctx": 3 - c}
        )

    def l_out(g):
        return remote(lsend.at[g], lrecv.at[g], l_send.at[g], l_recv.at[g], {"ctx": 3 - c})

    def q_out(j, t):
        land = qkv.at[j, t, rows_at(m * rows, rows)]
        return remote(land, land, q_send.at[j, t], q_recv.at[j, t], {"ctx": rim})

    lq_out = remote(lowt.at[m], lowt.at[m], lq_send.at[0], lq_recv.at[0], {"ctx": rim})
    og_out = remote(
        og_ref.at[pl.ds(0, hl), :], ogbuf.at[pl.ds(hl, hl), :], og_send.at[0], og_recv.at[0], {"ctx": lax.rem(c + 3, 4)}
    )

    def pos_out(k):
        return remote(pos_ref, posbuf.at[c], pos_send.at[k - 1], pos_recv.at[c], {"ctx": lax.rem(c + k, 4)})

    def o_out(j):
        return remote(osend.at[j], orecv.at[j], o_send.at[j], o_recv.at[j], {"ctx": lax.rem(c + 1, 4)})

    def gb_out(j, k):
        return remote(gbs.at[j], gbr.at[c, j], gb_send.at[j, k - 1], gb_recv.at[j, c], {"ctx": lax.rem(c + k, 4)})

    def tables():
        for block in range(4):

            @pl.when(block != c)
            def _():
                remote(pos_ref, posbuf.at[block], pos_send.at[0], pos_recv.at[block], {"sub": 1 - s}).wait_recv()

        own_pos.wait()
        lane = lax.broadcasted_iota(jnp.int32, (LANES, LANES), 1)
        half_dim = LANES // 2
        index = lax.broadcasted_iota(jnp.int32, (8, LANES), 1) % half_dim
        inverse = jnp.exp(index.astype(f32) * (-2.0 * math.log(10000.0) / HEAD_DIM))[0:1, :]

        def one(number, carry):
            place = lax.rem(4 * m + number + h, chunks)
            row = posbuf[place // 2, pl.ds(lax.rem(place, 2), 1), :].astype(f32)
            column = jnp.transpose(jnp.broadcast_to(row, (LANES, LANES)))
            angle = (column * (TRAIN_CTX / MAX_POS)) * inverse
            here = pl.ds(pl.multiple_of(number * LANES, LANES), LANES)
            ctab[here, :] = jnp.cos(angle)
            sine = jnp.sin(angle)
            stab[here, :] = jnp.where(lane < LANES // 2, -sine, sine)
            return carry

        lax.fori_loop(0, 4, one, 0)

    def turn(u, cosine, sine):
        return u * cosine + pltpu.roll(u, LANES // 2, 1) * sine

    scale = 1.0 / math.sqrt(HEAD_DIM)
    mine = rows_at((c - 2 * m) * rows, rows)

    def attend(j):
        here = cols(j, LANES)
        q, k, v, grad = qkv[j, 0, mine], qkv[j, 1, mine], qkv[j, 2, mine], ogbuf[:, here]
        allowed = lax.broadcasted_iota(jnp.int32, (rows, rows), 0) >= lax.broadcasted_iota(
            jnp.int32, (rows, rows), 1
        )
        scores = jnp.where(allowed, dot_t(q, k) * scale, -jnp.inf)
        highest = jnp.max(scores, axis=-1, keepdims=True)
        expo = jnp.exp(scores - highest)
        probs = expo * (1.0 / jnp.sum(expo, axis=-1, keepdims=True))
        probs_b = probs.astype(bf16)
        out = jnp.dot(probs_b, v, preferred_element_type=f32).astype(bf16)
        osend[j] = out[hl:]

        @pl.when(h == 0)
        def _():
            out_ref[:, here] = out

        @pl.when(h == 1)
        def _():
            o_out(j).start()
            out_ref[pl.ds(hl, hl), here] = out[:hl]

        dprob = dot_t(grad, v)
        delta = jnp.sum(grad.astype(f32) * out.astype(f32), axis=-1, keepdims=True)
        dscore_b = (probs * (dprob - delta) * scale).astype(bf16)
        dq = jnp.dot(dscore_b, k, preferred_element_type=f32)
        dq = turn(dq, ctab[mine, :], -stab[mine, :]).astype(bf16)
        dv = t_dot(probs_b, grad).astype(bf16)
        lgacc[...] += 2.0 * (dot_t(ball[0, :, here], dq) + dot_t(ball[2, :, here], dv))
        low = lowt[c - 2 * m]
        gbs[j, 0:8, :] = (2.0 * jnp.dot(low, dq, preferred_element_type=f32))[0:8]
        gbs[j, 8:16, :] = (2.0 * jnp.dot(low, dv, preferred_element_type=f32))[8:16]
        for k_ in range(1, 4):
            gb_out(j, k_).start()

    def reach_two():
        pl.semaphore_wait(second_sem, beside)
        greet(third_sem)

    def reach_three():
        pl.semaphore_wait(third_sem, beside)
        for k in range(1, 4):
            pos_out(k).start()

    def factors_in():
        for copy in factors:
            copy.wait()
        nothing = jnp.zeros((8, 4 * LANES), f32)
        ball[0] = jnp.concatenate([bqbuf[...].astype(f32), nothing], axis=0).astype(bf16)
        ball[1] = jnp.concatenate([nothing, nothing], axis=0).astype(bf16)
        ball[2] = jnp.concatenate([nothing, bvbuf[...].astype(f32)], axis=0).astype(bf16)
        lgacc[...] = jnp.zeros(lgacc.shape, f32)

    def og_in():
        @pl.when(h == 1)
        def _():
            og_out.wait_recv()
            own_og[1].wait()

        @pl.when(h == 0)
        def _():
            own_og[0].wait()
            own_og[1].wait()

    @pl.when(inner)
    def _():
        e = jnp.where(home, 1, 0)

        @pl.when(home)
        def _():
            for half in range(2):
                for p in range(NP):
                    h_twin(c, half, p, own_piece(half, p)).start()

        @pl.when(away)
        def _():
            for p in range(NP):
                h_relay_in(p).start()
                h_direct(p).start()

        def z_in(b, p):
            h_arrived(b, e, p, s).wait_recv()
            h_cross(b, e, p).start()
            h_twin(b, e, p).start()

        def x_in(b, half, p):
            h_arrived(b, half, p, s).wait_recv()
            h_twin(b, half, p).start()

        def twin_in(b):
            for half in range(2):
                for p in range(NP):
                    h_arrived(b, half, p, 1 - s).wait_recv()

        def forward(j, t):
            for w in range(WP):
                copy = w_pass(j, t, w)
                copy.wait_recv()
                copy.start()

        def passed(j, t):
            for w in range(WP):
                w_arrived(j, t, w).wait_recv()

        def group_rows(g):
            return rows_at(g * rows, rows)

        def side_rows(side):
            return rows_at(side * 2 * rows, 2 * rows)

        def partner(j, t, g):
            here = half_of(g, 1 - m)
            group = jnp.where(g == 0, 3 - c, 3 * (1 - m))
            y = jnp.dot(hbuf[group_rows(group), :], wbuf[j, t], preferred_element_type=f32)
            psend[j, t, here] = y.astype(bf16)
            p_out(j, t, g).start()

        def partner_both(j, t):
            y = jnp.dot(hbuf[side_rows(1 - m), :], wbuf[j, t], preferred_element_type=f32)
            psend[j, t] = y.astype(bf16)
            p_out(j, t, 1).start()
            p_out(j, t, 0).start()

        whole = [(half, p) for half in range(2) for p in range(NP)]
        pieces = [(t, w) for t in range(3) for w in range(WP)]
        rest = list(pieces)

        def forward_piece(j, t, w):
            copy = w_pass(j, t, w)
            copy.wait_recv()
            copy.start()

        for p in range(NP):

            @pl.when(home)
            def _():
                h_relay_in(p).wait_recv()
                h_relay_out(p).start()

            if p == 0:
                reach_two()
            z_in(3 - c, p)
            if p == 0:
                reach_three()
            forward_piece(0, *rest.pop(0))

        @pl.when(home)
        def _():
            for half, p in whole[:2]:
                h_cross(c, half, p, own_piece(half, p)).start()

        while rest:
            forward_piece(0, *rest.pop(0))
        pl.when(h == 1)(og_out.start)
        far = 3 * (1 - m)
        late = (c == 1) & (h == 1)

        def first_in(t, carry):
            partner(0, t, 0)
            return carry

        def first_out(t, carry):
            partner(0, t, 1)
            return carry

        for p in range(NP // 2):
            z_in(far, p)
        for p in range(NP):
            x_in(3 - c, 1 - e, p)
            if p + NP // 2 < NP - 1:
                z_in(far, p + NP // 2)
        twin_in(3 - c)

        @pl.when(home)
        def _():
            for copy in own_h:
                copy.wait()
            twin_in(c)

        for t in range(3):
            own_w(0, t).wait()
            passed(0, t)

        @pl.when(jnp.logical_not(late))
        def _():
            lax.fori_loop(0, 3, first_in, 0)

        z_in(far, NP - 1)
        factors_in()
        tables()
        for p in range(NP):
            z_in(rim, p)
            x_in(far, 1 - e, p)

        @pl.when(home)
        def _():
            for half, p in whole[2:]:
                h_cross(c, half, p, own_piece(half, p)).start()

        twin_in(far)

        @pl.when(late)
        def _():
            lax.fori_loop(0, 3, first_in, 0)

        @pl.when(jnp.logical_not(late))
        def _():
            lax.fori_loop(0, 3, first_out, 0)

        forward(1, 0)
        for p in range(NP):
            x_in(rim, 1 - e, p)
        twin_in(rim)

        @pl.when(late)
        def _():
            lax.fori_loop(0, 3, first_out, 0)

        for j in range(1, 4):
            for t in range(3):
                own_w(j, t).wait()
        a_both = jnp.concatenate(
            [
                aqbuf[:, pl.ds(pl.multiple_of(m * 2 * width, LANES), 2 * width)].astype(f32),
                avbuf[:, pl.ds(pl.multiple_of(m * 2 * width, LANES), 2 * width)].astype(f32),
            ],
            axis=0,
        ).astype(bf16)

        def low_other(g, carry):
            group = 2 * (1 - m) + g
            lsend[g] = dot_t(a_both, hbuf[group_rows(group), :])
            l_out(g).start()
            return carry

        forward(1, 1)
        lax.fori_loop(0, 2, low_other, 0)

        def low_own(g, carry):
            group = 2 * m + g
            l_out(g).wait_recv()
            lowt[g] = (dot_t(a_both, hbuf[group_rows(group), :]) + lrecv[g]).astype(bf16)
            return carry

        def finish(i):
            j, t = i // 3, lax.rem(i, 3)
            plain = t == 2

            low = jnp.concatenate([lowt[0], lowt[1]], axis=1)
            y = jnp.dot(hbuf[side_rows(m), :], wbuf[j, t], preferred_element_type=f32)
            y = y + 2.0 * t_dot(low, ball[t, :, cols(j, LANES)])
            cosine = jnp.where(plain, 1.0, ctab[...])
            sine = jnp.where(plain, 0.0, stab[...])
            for g in (1, 0):
                p_out(j, t, g, m).wait_recv()
            qkv[j, t] = turn(y + precv[j, t].astype(f32), cosine, sine).astype(bf16)
            q_out(j, t).start()

        def slot(i, carry):
            @pl.when(i < 13)
            def _():
                j, t = (i - 1) // 3, lax.rem(i - 1, 3)
                passed(j, t)

                partner_both(j, t)

            @pl.when(i < 11)
            def _():
                forward((i + 1) // 3, lax.rem(i + 1, 3))

            @pl.when(i == 6)
            def _():
                @pl.when(away)
                def _():
                    for half, p in whole:
                        x_in(c, half, p)
                    twin_in(c)

                lax.fori_loop(0, 2, low_own, 0)
                lq_out.start()

            first = jnp.where(i == 6, 0, jnp.where(i == 7, 2, i - 4))
            count = jnp.where(i < 6, 0, jnp.where(i < 8, 2, 1))

            def some(k, carry_):
                finish(first + k)
                return carry_

            lax.fori_loop(0, count, some, 0)

            pl.when(i == 7)(og_in)

            @pl.when((i == 7) | (i == 9) | (i == 12) | (i == 15))
            def _():
                attend(jnp.where(i == 15, 3, (i - 6) // 2 - jnp.where(i == 12, 1, 0)))

            return carry

        lax.fori_loop(4, 16, slot, 0)

    @pl.when(outer)
    def _():
        for t in range(3):
            for w in range(WP):
                w_out(0, t, w).start()
        for p in range(NP):
            h_relay_in(p).start()
        reach_two()
        reach_three()

        def relays():
            for p in range(NP):
                h_relay_in(p).wait_recv()
                h_relay_out(p).start()

        @pl.when(home)
        def _():
            relays()
            for p in range(NP):
                h_direct(p).start()

        @pl.when(away)
        def _():
            for p in range(NP):
                h_direct(p).start()
            relays()

        def send_w(j, carry):
            for t in range(3):
                for w in range(WP):
                    remote(
                        weights[t].at[rows_at(r * (depth // 2) + w * wrows, wrows), cols(j, LANES)],
                        wslot(j, t, c - 2 * m, r, w),
                        w_send.at[j, t, w],
                        w_recv.at[j, t, r, w],
                        {"ctx": near},
                    ).start()
            return carry

        send_w(1, 0)
        pl.when(h == 1)(og_out.start)
        lax.fori_loop(2, 4, send_w, 0)
        factors_in()
        tables()
        og_in()
        remote(lowt.at[m], lowt.at[m], lq_send.at[0], lq_recv.at[0], {"sub": 1 - s}).wait_recv()

        def one(j, carry):
            for t in range(3):
                q_out(j, t).wait_recv()
            attend(j)
            return carry

        lax.fori_loop(0, 4, one, 0)

    lgs[...] = lgacc[...].astype(bf16)
    lgr[me] = lgs[...]

    def lg_out(k):
        dest = 4 + k
        return remote(lgs, lgr.at[me], lg_send.at[k], lg_recv.at[me], member(dest))

    for k in range(8):
        pl.when(me != 4 + k)(lg_out(k).start)

    for p in range(NP):
        pl.when(direct_on)(h_direct(p).wait_send)
        pl.when(direct_on)(h_relay_in(p).wait_send)
        pl.when(relay_on)(h_relay_out(p).wait_send)
    for k in range(1, 4):
        pos_out(k).wait_send()
    pl.when(h == 1)(og_out.wait_send)

    @pl.when(outer)
    def _():
        for j in range(4):
            for t in range(3):
                for w in range(WP):
                    w_out(j, t, w).wait_send()

    @pl.when(inner)
    def _():
        for b in range(4):
            for half in range(2):
                for p in range(NP):
                    h_twin(b, half, p).wait_send()
                    crossed = ((b == c) & home) | ((b != c) & (home == (half == 1)))
                    pl.when(crossed)(h_cross(b, half, p).wait_send)
        for j in range(4):
            for t in range(3):
                for w in range(WP):
                    w_pass(j, t, w).wait_send()
                for g in range(2):
                    p_out(j, t, g).wait_send()
                q_out(j, t).wait_send()
        for g in range(2):
            l_out(g).wait_send()
        lq_out.wait_send()

    def ga_out(k):
        dest = lax.rem(me + k, 16)
        return remote(gas, gar.at[me - 4], ga_send.at[k - 1], ga_recv.at[me - 4], member(dest))

    @pl.when(inner)
    def _():
        for k in range(1, 16):
            frm = lax.rem(me + k, 16)
            remote(lgs, lgr.at[frm], lg_send.at[0], lg_recv.at[frm], {"sub": 1 - s}).wait_recv()

        def side(hd):
            return jnp.concatenate(
                [
                    lgr[4 * g + 2 * hd].astype(f32) + lgr[4 * g + 2 * hd + 1].astype(f32)
                    for g in range(4)
                ],
                axis=1,
            )

        zero, one = side(0), side(1)
        wide_ = 4 * rows
        right = jnp.concatenate([one[:, wide_ - hl :], one[:, : wide_ - hl]], axis=1)
        left = jnp.concatenate([zero[:, hl:], zero[:, :hl]], axis=1)
        low = jnp.where(h == 0, zero + right, left + one)
        upper = low.astype(bf16)
        lower = (low - upper.astype(f32)).astype(bf16)
        both = jnp.concatenate([upper, lower], axis=0)
        part_ = jnp.dot(both, hbuf[:, cols(h * 2 + s, slice_k)], preferred_element_type=f32)
        gas[...] = (part_[0:16] + part_[16:32]).astype(bf16)
        gar[me - 4] = gas[...]
        for k in range(1, 16):
            ga_out(k).start()

    @pl.when(h == 1)
    def _():
        for j in range(4):
            o_out(j).wait_recv()
            out_ref[0:hl, j * LANES : (j + 1) * LANES] = orecv[j]

    for j in range(4):
        for block in range(4):

            @pl.when(block != c)
            def _():
                remote(gbs.at[0], gbr.at[block, j], gb_send.at[0, 0], gb_recv.at[j, block], {"sub": 1 - s}).wait_recv()

        gbr[c, j] = gbs[j]
        total = (gbr[0, j] + gbr[1, j]) + (gbr[2, j] + gbr[3, j])
        gbq_ref[:, j * LANES : (j + 1) * LANES] = total[0:8]
        gbv_ref[:, j * LANES : (j + 1) * LANES] = total[8:16]

    for k in range(8):

        @pl.when(me != 4 + k)
        def _():
            remote(gas, gar.at[k], ga_send.at[0], ga_recv.at[k], {"sub": 1 - s}).wait_recv()

        block = gar[k].astype(f32)
        gaq_ref[:, k * slice_k : (k + 1) * slice_k] = block[0:8]
        gav_ref[:, k * slice_k : (k + 1) * slice_k] = block[8:16]

    @pl.when(h == 1)
    def _():
        for j in range(4):
            o_out(j).wait_send()

    for j in range(4):
        for k in range(1, 4):
            gb_out(j, k).wait_send()
    for k in range(8):
        pl.when(me != 4 + k)(lg_out(k).wait_send)

    @pl.when(inner)
    def _():
        for k in range(1, 16):
            ga_out(k).wait_send()


def hand_over_kernel(count, *refs):
    sources, results, stages, sems = refs[:count], refs[count : 2 * count], refs[2 * count : 3 * count], refs[-1]
    fetched = [pltpu.make_async_copy(sources[k], stages[k], sems.at[0, k]) for k in range(count)]
    stored = [pltpu.make_async_copy(stages[k], results[k], sems.at[1, k]) for k in range(count)]
    for copy in fetched:
        copy.start()
    for k in reversed(range(count)):
        fetched[k].wait()
        stored[k].start()
    for copy in stored:
        copy.wait()


def hand_over(*arrays):
    spec = pl.BlockSpec(memory_space=pl.ANY)
    count = len(arrays)
    return pl.pallas_call(
        functools.partial(hand_over_kernel, count),
        out_shape=tuple(jax.ShapeDtypeStruct(a.shape, a.dtype) for a in arrays),
        in_specs=[spec] * count,
        out_specs=[spec] * count,
        scratch_shapes=[pltpu.VMEM(a.shape, a.dtype) for a in arrays] + [pltpu.SemaphoreType.DMA((2, count))],
    )(*arrays)


def paired(
    hidden_states, w_query, w_key, w_value, a_query, a_value, b_query, b_value, positions, out_grad
):
    f32, bf16 = jnp.float32, jnp.bfloat16
    rows, width = hidden_states.shape
    model, rank = a_query.shape
    depth, columns = w_query.shape
    pos = positions.reshape(rows // LANES, LANES)
    vmem, dma = pltpu.VMEM, pltpu.SemaphoreType.DMA
    hbm_spec = pl.BlockSpec(memory_space=pl.ANY)
    vmem_spec = pl.BlockSpec(memory_space=pltpu.VMEM)
    out, gaq, gbq, gav, gbv = pl.pallas_call(
        paired_kernel,
        out_shape=(
            jax.ShapeDtypeStruct((rows, columns), bf16),
            jax.ShapeDtypeStruct((rank, model), f32),
            jax.ShapeDtypeStruct((rank, columns), f32),
            jax.ShapeDtypeStruct((rank, model), f32),
            jax.ShapeDtypeStruct((rank, columns), f32),
        ),
        in_specs=[hbm_spec] * 10,
        out_specs=[vmem_spec] * 5,
        scratch_shapes=[
            vmem((4 * rows, 2 * width), bf16),
            vmem((4, 3, 2 * depth, LANES), bf16),
            vmem((rows // 2, width), bf16),
            vmem((4, 3, 2 * rows, LANES), bf16),
            vmem((4, 3, 2 * rows, LANES), bf16),
            vmem((2, 16, rows), f32),
            vmem((2, 16, rows), f32),
            vmem((4, 3, 2 * rows, LANES), bf16),
            vmem((2, 16, rows), bf16),
            vmem((3, 16, columns), bf16),
            vmem((rows, columns), bf16),
            vmem((4, rows // LANES, LANES), jnp.int32),
            vmem((2 * rows, LANES), f32),
            vmem((2 * rows, LANES), f32),
            vmem((4, rows // 2, LANES), bf16),
            vmem((4, rows // 2, LANES), bf16),
            vmem((4, 16, LANES), f32),
            vmem((4, 4, 16, LANES), f32),
            vmem((16, rows), f32),
            vmem((16, rows), bf16),
            vmem((16, 16, rows), bf16),
            vmem((16, model // 8), bf16),
            vmem((8, 16, model // 8), bf16),
            vmem((rank, model), bf16),
            vmem((rank, model), bf16),
            vmem((rank, columns), bf16),
            vmem((rank, columns), bf16),
            pltpu.SemaphoreType.REGULAR,
            pltpu.SemaphoreType.REGULAR,
            dma((21,)),
            dma((2, NP)),
            dma((NP,)),
            dma((NP,)),
            dma((4, 2, NP)),
            dma((4, 2, NP)),
            dma((4, 2, NP, 2)),
            dma((4, 3, WP)),
            dma((4, 3, WP)),
            dma((4, 3, 2, WP)),
            dma((4, 3, 2)),
            dma((4, 3, 2)),
            dma((2,)),
            dma((2,)),
            dma((4, 3)),
            dma((4, 3)),
            dma((1,)),
            dma((1,)),
            dma((1,)),
            dma((1,)),
            dma((3,)),
            dma((4,)),
            dma((4,)),
            dma((4,)),
            dma((4, 3)),
            dma((4, 4)),
            dma((8,)),
            dma((16,)),
            dma((15,)),
            dma((8,)),
        ],
        compiler_params=pltpu.CompilerParams(
            collective_id=1, has_side_effects=True, vmem_limit_bytes=56 * 1024 * 1024
        ),
    )(
        hidden_states, w_query, w_key, w_value, a_query.T, a_value.T, b_query, b_value, pos, out_grad
    )
    out, gaq, gbq, gav, gbv = hand_over(out, gaq, gbq, gav, gbv)
    return (out, gaq.T, gbq, gav.T, gbv)


def fits_paired(mesh, args):
    hidden_states, w_query, a_query = args[0], args[1], args[4]
    return (
        mesh.shape["rep"] == 2
        and mesh.shape["ctx"] == 4
        and mesh.shape["head"] == 2
        and mesh.shape["sub"] == 2
        and w_query.shape[1] == 4 * HEAD_DIM
        and HEAD_DIM == LANES
        and HEADS == 16
        and a_query.shape[1] == 8
        and hidden_states.shape[0] == 2 * LANES
        and hidden_states.shape[1] == w_query.shape[0]
        and a_query.shape[0] == 4 * w_query.shape[0]
        and w_query.shape[0] == 1024
    )


def choose(mesh, *args):
    return paired(*args) if fits_paired(mesh, args) else local(*args)


def solution(mesh):
    in_specs = (
        P(("rep", "ctx"), ("head", "sub")),
        P("ctx", ("head", "sub")),
        P("ctx", ("head", "sub")),
        P("ctx", ("head", "sub")),
        P(),
        P(),
        P(None, ("head", "sub")),
        P(None, ("head", "sub")),
        P(("rep", "ctx")),
        P(("rep", "ctx"), ("head", "sub")),
    )
    out_specs = (
        P(("rep", "ctx"), ("head", "sub")),
        P(None, "rep"),
        P("rep", ("head", "sub")),
        P(None, "rep"),
        P("rep", ("head", "sub")),
    )
    return jax.shard_map(
        functools.partial(choose, mesh), mesh=mesh, in_specs=in_specs, out_specs=out_specs, check_vma=False
    )
```

```python
import functools
import math

import jax
import jax.numpy as jnp
from jax import lax
from jax.experimental import pallas as pl
from jax.experimental.pallas import tpu as pltpu
from jax.sharding import PartitionSpec as P

HEAD_DIM = 128
HEADS = 16
TRAIN_CTX = 4096
MAX_POS = 100000


def passed_along(block, axis, distance):
    devices = range(lax.axis_size(axis))
    route = [((i - distance) % len(devices), i) for i in devices]
    return lax.ppermute(block, axis, route)


def rope_tables(positions):
    half_dim = HEAD_DIM // 2
    inverse = jnp.exp(
        jnp.arange(half_dim, dtype=jnp.float32) * (-2.0 * math.log(10000.0) / HEAD_DIM)
    )
    scaled = positions.astype(jnp.float32) * (TRAIN_CTX / MAX_POS)
    angle = scaled[:, None] * inverse[None, :]
    return (jnp.cos(angle)[:, None, :], jnp.sin(angle)[:, None, :])


def rotate(vectors, cosine, sine):
    half_dim = vectors.shape[-1] // 2
    first = vectors[..., :half_dim]
    second = vectors[..., half_dim:]
    return jnp.concatenate(
        [first * cosine - second * sine, second * cosine + first * sine], axis=-1
    )


def project_back(features, low_grads):
    block_width = min(features.shape[1], 512)
    block_count = features.shape[1] // block_width

    def one_block(number):
        section = lax.dynamic_slice_in_dim(features, number * block_width, block_width, 1).astype(
            jnp.float32
        )
        return lax.dot_general(
            section, low_grads, (((0,), (0,)), ((), ())), precision=lax.Precision.HIGHEST
        )

    blocks = lax.map(one_block, jnp.arange(block_count))
    return blocks.reshape(features.shape[1], low_grads.shape[1])


def local(
    hidden_states, w_query, w_key, w_value, a_query, a_value, b_query, b_value, positions, out_grad
):
    rows_here = hidden_states.shape[0]
    columns = w_query.shape[1]
    heads_here = columns // HEAD_DIM
    rank_cols = a_query.shape[1]
    scale = 1.0 / math.sqrt(HEAD_DIM)
    shard_count = lax.axis_size("ctx")
    total_tokens = rows_here * shard_count
    group_len = total_tokens // 4
    reach = (group_len // 2 % rows_here + group_len - 1) // rows_here
    full_states = lax.all_gather(hidden_states, ("head", "sub"), axis=1, tiled=True)
    pieces = (
        lax.all_gather(w_query, "ctx", axis=0, tiled=True),
        lax.all_gather(w_key, "ctx", axis=0, tiled=True),
        lax.all_gather(w_value, "ctx", axis=0, tiled=True),
    )
    base_q, base_k, base_v = tuple(
        (
            jnp.dot(full_states, weights_piece, preferred_element_type=jnp.float32)
            for weights_piece in pieces
        )
    )
    low_q = jnp.dot(full_states, a_query, preferred_element_type=jnp.float32).astype(jnp.bfloat16)
    low_v = jnp.dot(full_states, a_value, preferred_element_type=jnp.float32).astype(jnp.bfloat16)
    cosine, sine = rope_tables(positions)
    pre_q = base_q + 2.0 * jnp.dot(low_q, b_query, preferred_element_type=jnp.float32)
    queries = rotate(pre_q.reshape(rows_here, heads_here, HEAD_DIM), cosine, sine).astype(
        jnp.bfloat16
    )
    keyed = rotate(base_k.reshape(rows_here, heads_here, HEAD_DIM), cosine, sine).astype(
        jnp.bfloat16
    )
    valued = (base_v + 2.0 * jnp.dot(low_v, b_value, preferred_element_type=jnp.float32)).astype(
        jnp.bfloat16
    )
    valued = valued.reshape(rows_here, heads_here, HEAD_DIM)
    current = jnp.stack([keyed, valued])
    collected = [current]
    for level in range(reach):
        current = passed_along(current, "ctx", 1)
        collected.append(current)
    key_rows = jnp.concatenate([block[0] for block in collected], axis=0)
    value_rows = jnp.concatenate([block[1] for block in collected], axis=0)
    shard_id = lax.axis_index("ctx")
    head_ids = lax.axis_index(("head", "sub")) * heads_here + jnp.arange(heads_here)
    amount = jnp.where(head_ids >= HEADS // 2, group_len // 2, 0).astype(jnp.int32)
    query_pos = shard_id * rows_here + jnp.arange(rows_here, dtype=jnp.int32)
    block_ids = jnp.arange(reach + 1, dtype=jnp.int32)
    source_shard = (shard_id - block_ids) % shard_count
    key_pos = (
        source_shard[:, None] * rows_here + jnp.arange(rows_here, dtype=jnp.int32)[None, :]
    ).reshape(-1)
    query_num = (query_pos[None, :] - amount[:, None]) % total_tokens
    key_num = (key_pos[None, :] - amount[:, None]) % total_tokens
    same_group = key_num[:, None, :] // group_len == query_num[:, :, None] // group_len
    visible = same_group & (key_num[:, None, :] <= query_num[:, :, None])
    scores = (
        jnp.einsum("qhd,khd->hqk", queries, key_rows, preferred_element_type=jnp.float32) * scale
    )
    scores = jnp.where(visible, scores, -jnp.inf)
    highest = jnp.max(scores, axis=-1, keepdims=True)
    expo = jnp.where(visible, jnp.exp(scores - highest), 0.0)
    probs = expo / jnp.sum(expo, axis=-1, keepdims=True)
    probs_b = probs.astype(jnp.bfloat16)
    attended = jnp.einsum("hqk,khd->qhd", probs_b, value_rows, preferred_element_type=jnp.float32)
    attn_out = attended.astype(jnp.bfloat16)
    grads = out_grad.reshape(rows_here, heads_here, HEAD_DIM)
    dprob = jnp.einsum("qhd,khd->hqk", grads, value_rows, preferred_element_type=jnp.float32)
    delta = jnp.sum(grads.astype(jnp.float32) * attn_out.astype(jnp.float32), axis=-1)
    dscore = probs * (dprob - delta.T[:, :, None])
    dscore_b = (dscore * scale).astype(jnp.bfloat16)
    dquery = jnp.einsum("hqk,khd->qhd", dscore_b, key_rows, preferred_element_type=jnp.float32)
    dvalue = jnp.einsum("hqk,qhd->khd", probs_b, grads, preferred_element_type=jnp.float32)
    value_blocks = dvalue.reshape(reach + 1, rows_here, columns)
    carried = value_blocks[reach]
    for level in range(reach, 0, -1):
        carried = passed_along(carried, "ctx", -1) + value_blocks[level - 1]
    dv_local = carried.astype(jnp.bfloat16)
    dq_local = rotate(dquery, cosine, -sine).astype(jnp.bfloat16).reshape(rows_here, columns)
    grad_bq = 2.0 * jnp.dot(low_q.T, dq_local, preferred_element_type=jnp.float32)
    grad_bv = 2.0 * jnp.dot(low_v.T, dv_local, preferred_element_type=jnp.float32)
    low_grads = jnp.concatenate(
        [
            2.0 * jnp.dot(dq_local, b_query.T, preferred_element_type=jnp.float32),
            2.0 * jnp.dot(dv_local, b_value.T, preferred_element_type=jnp.float32),
        ],
        axis=1,
    )
    grad_down = lax.psum(project_back(full_states, low_grads), ("ctx", "head", "sub"))
    grad_bq, grad_bv = lax.psum((grad_bq, grad_bv), "ctx")
    return (
        attn_out.reshape(rows_here, columns),
        grad_down[:, :rank_cols],
        grad_bq,
        grad_down[:, rank_cols:],
        grad_bv,
    )


LANES = 128
MESH = pl.DeviceIdType.MESH
NP = 4
WP = 2


def paired_kernel(
    hid_ref,
    wq_ref,
    wk_ref,
    wv_ref,
    aq_ref,
    av_ref,
    bq_ref,
    bv_ref,
    pos_ref,
    og_ref,
    out_ref,
    gaq_ref,
    gbq_ref,
    gav_ref,
    gbv_ref,
    hbuf,
    wbuf,
    relay,
    psend,
    precv,
    lsend,
    lrecv,
    qkv,
    held,
    lowt,
    ball,
    ogbuf,
    posbuf,
    ctab,
    stab,
    osend,
    orecv,
    gbs,
    gbr,
    lgacc,
    lgs,
    lgr,
    gas,
    gar,
    aqbuf,
    avbuf,
    bqbuf,
    bvbuf,
    second_sem,
    third_sem,
    local_sem,
    hz_send,
    hxr_send,
    rl_recv,
    hx_send,
    hs_send,
    h_recv,
    w_send,
    wy_send,
    w_recv,
    p_send,
    p_recv,
    l_send,
    l_recv,
    q_send,
    q_recv,
    lq_send,
    lq_recv,
    og_send,
    og_recv,
    pos_send,
    pos_recv,
    o_send,
    o_recv,
    gb_send,
    gb_recv,
    lg_send,
    lg_recv,
    ga_send,
    ga_recv,
):
    f32, bf16 = jnp.float32, jnp.bfloat16
    rows, width = hid_ref.shape
    depth = wq_ref.shape[0]
    hl = rows // 2
    pr = hl // NP
    wrows = depth // (2 * WP)
    chunks = 2 * 4
    slice_k = 2 * width // 4
    r, c = lax.axis_index("rep"), lax.axis_index("ctx")
    h, s = lax.axis_index("head"), lax.axis_index("sub")
    m = c // 2
    inner = (c == 1) | (c == 2)
    outer = (c == 0) | (c == 3)
    near = 1 + m
    far_c = 3 - c
    rim = 3 * m
    home = h == m
    away = h != m
    me = c * 4 + h * 2 + s
    weights = (wq_ref, wk_ref, wv_ref)
    dot_t = functools.partial(
        lax.dot_general, dimension_numbers=(((1,), (1,)), ((), ())), preferred_element_type=f32
    )
    t_dot = functools.partial(
        lax.dot_general, dimension_numbers=(((0,), (0,)), ((), ())), preferred_element_type=f32
    )

    def member(number):
        hs = lax.rem(number, 4)
        return {"ctx": number // 4, "head": hs // 2, "sub": lax.rem(hs, 2)}

    def remote(src, dst, send, recv, device):
        return pltpu.make_async_remote_copy(
            src_ref=src, dst_ref=dst, send_sem=send, recv_sem=recv, device_id=device, device_id_type=MESH
        )

    def rows_at(start, size):
        return pl.ds(pl.multiple_of(start, 16), size)

    def cols(number, size):
        return pl.ds(pl.multiple_of(number * size, LANES), size)

    barrier = pltpu.get_barrier_semaphore()

    def greet(semaphore):
        for cond, device in ((c > 0, {"ctx": c - 1}), (c < 3, {"ctx": c + 1})):

            @pl.when(cond)
            def _():
                pl.semaphore_signal(semaphore, inc=1, device_id=device, device_id_type=MESH)

    greet(barrier)
    for axis, place in (("head", h), ("sub", s), ("rep", r)):
        pl.semaphore_signal(barrier, inc=1, device_id={axis: 1 - place}, device_id_type=MESH)

    def own_piece(e, p):
        return hid_ref.at[pl.ds(e * hl + p * pr, pr), :]

    def chunk_of(b, e, hd):
        return lax.rem(2 * b + e - hd + chunks, chunks)

    def hslot(b, e, p, hd, q):
        return hbuf.at[rows_at(chunk_of(b, e, hd) * hl + p * pr, pr), cols(q, width)]

    def wslot(j, t, quarter, side, w):
        return wbuf.at[j, t, rows_at(quarter * depth + side * (depth // 2) + w * wrows, wrows), :]

    own_h = [
        pltpu.make_async_copy(
            hid_ref.at[pl.ds(e * hl, hl), :],
            hbuf.at[rows_at(chunk_of(c, e, h) * hl, hl), cols(s, width)],
            local_sem.at[e],
        )
        for e in range(2)
    ]
    own_pos = pltpu.make_async_copy(pos_ref, posbuf.at[c], local_sem.at[2])
    own_og = [
        pltpu.make_async_copy(og_ref.at[pl.ds(0, hl), :], ogbuf.at[pl.ds(0, hl), :], local_sem.at[3]),
        pltpu.make_async_copy(
            og_ref.at[pl.ds(hl, hl), :], ogbuf.at[rows_at(hl - h * hl, hl), :], local_sem.at[4]
        ),
    ]

    def own_w(j, t):
        return pltpu.make_async_copy(
            weights[t].at[:, pl.ds(j * LANES, LANES)],
            wbuf.at[j, t, rows_at((c - 2 * m) * depth, depth), :],
            local_sem.at[5 + 3 * j + t],
        )

    factors = [
        pltpu.make_async_copy(src, dst, local_sem.at[17 + k])
        for k, (src, dst) in enumerate(
            ((aq_ref, aqbuf), (av_ref, avbuf), (bq_ref, bqbuf), (bv_ref, bvbuf))
        )
    ]
    for copy in factors:
        copy.start()
    own_pos.start()

    @pl.when(inner & home)
    def _():
        for copy in own_h:
            copy.start()

    @pl.when(inner)
    def _():
        for j in range(4):
            for t in range(3):
                own_w(j, t).start()

    own_og[1].start()
    pl.when(h == 0)(own_og[0].start)
    beside = jnp.where(inner, 2, 1)
    pl.semaphore_wait(barrier, 3 + beside)
    greet(second_sem)

    def h_direct(p):
        return remote(own_piece(1, p), hslot(c, 1, p, h, s), hz_send.at[0, p], h_recv.at[c, 1, p, s], {"ctx": 1 + h})

    def h_relay_in(p):
        return remote(
            own_piece(0, p), relay.at[pl.ds(p * pr, pr), :], hxr_send.at[p], rl_recv.at[p], {"head": 1 - h}
        )

    def h_relay_out(p):
        return remote(
            relay.at[pl.ds(p * pr, pr), :],
            hslot(c, 0, p, h, s),
            hz_send.at[1, p],
            h_recv.at[c, 0, p, s],
            {"ctx": 2 - h},
        )

    direct_on = c != 1 + h
    relay_on = c != 2 - h

    def h_cross(b, e, p, src=None):
        return remote(
            hslot(b, e, p, h, s) if src is None else src,
            hslot(b, e, p, 1 - h, s),
            hx_send.at[b, e, p],
            h_recv.at[b, e, p, s],
            {"head": 1 - h},
        )

    def h_twin(b, e, p, src=None):
        land = hslot(b, e, p, h, s)
        return remote(
            land if src is None else src, land, hs_send.at[b, e, p], h_recv.at[b, e, p, s], {"sub": 1 - s}
        )

    def h_arrived(b, e, p, q):
        land = hslot(b, e, p, h, q)
        return remote(land, land, hx_send.at[0, 0, 0], h_recv.at[b, e, p, q], {"sub": 1 - s})

    def w_out(j, t, w):
        return remote(
            weights[t].at[rows_at(r * (depth // 2) + w * wrows, wrows), pl.ds(j * LANES, LANES)],
            wslot(j, t, c - 2 * m, r, w),
            w_send.at[j, t, w],
            w_recv.at[j, t, r, w],
            {"ctx": near},
        )

    other = 1 - (c - 2 * m)

    def w_pass(j, t, w):
        land = wslot(j, t, other, r, w)
        return remote(land, land, wy_send.at[j, t, w], w_recv.at[j, t, r, w], {"rep": 1 - r})

    def w_arrived(j, t, w):
        land = wslot(j, t, other, 1 - r, w)
        return remote(land, land, wy_send.at[0, 0, 0], w_recv.at[j, t, 1 - r, w], {"rep": 1 - r})

    def half_of(g, side):
        return rows_at(jnp.where(g == 0, 1 - side, side) * rows, rows)

    def p_out(j, t, g, side=None):
        here = half_of(g, 1 - m if side is None else side)
        return remote(
            psend.at[j, t, here], precv.at[j, t, here], p_send.at[j, t, g], p_recv.at[j, t, g], {"ctx": 3 - c}
        )

    def l_out(g):
        return remote(lsend.at[g], lrecv.at[g], l_send.at[g], l_recv.at[g], {"ctx": 3 - c})

    def q_out(j, t):
        land = qkv.at[j, t, rows_at(m * rows, rows)]
        return remote(land, land, q_send.at[j, t], q_recv.at[j, t], {"ctx": rim})

    lq_out = remote(lowt.at[m], lowt.at[m], lq_send.at[0], lq_recv.at[0], {"ctx": rim})
    og_out = remote(
        og_ref.at[pl.ds(0, hl), :], ogbuf.at[pl.ds(hl, hl), :], og_send.at[0], og_recv.at[0], {"ctx": lax.rem(c + 3, 4)}
    )

    def pos_out(k):
        return remote(pos_ref, posbuf.at[c], pos_send.at[k - 1], pos_recv.at[c], {"ctx": lax.rem(c + k, 4)})

    def o_out(j):
        return remote(osend.at[j], orecv.at[j], o_send.at[j], o_recv.at[j], {"ctx": lax.rem(c + 1, 4)})

    def gb_out(j, k):
        return remote(gbs.at[j], gbr.at[c, j], gb_send.at[j, k - 1], gb_recv.at[j, c], {"ctx": lax.rem(c + k, 4)})

    def tables():
        for block in range(4):

            @pl.when(block != c)
            def _():
                remote(pos_ref, posbuf.at[block], pos_send.at[0], pos_recv.at[block], {"sub": 1 - s}).wait_recv()

        own_pos.wait()
        lane = lax.broadcasted_iota(jnp.int32, (LANES, LANES), 1)
        half_dim = LANES // 2
        index = lax.broadcasted_iota(jnp.int32, (8, LANES), 1) % half_dim
        inverse = jnp.exp(index.astype(f32) * (-2.0 * math.log(10000.0) / HEAD_DIM))[0:1, :]

        def one(number, carry):
            place = lax.rem(4 * m + number + h, chunks)
            row = posbuf[place // 2, pl.ds(lax.rem(place, 2), 1), :].astype(f32)
            column = jnp.transpose(jnp.broadcast_to(row, (LANES, LANES)))
            angle = (column * (TRAIN_CTX / MAX_POS)) * inverse
            here = pl.ds(pl.multiple_of(number * LANES, LANES), LANES)
            ctab[here, :] = jnp.cos(angle)
            sine = jnp.sin(angle)
            stab[here, :] = jnp.where(lane < LANES // 2, -sine, sine)
            return carry

        lax.fori_loop(0, 4, one, 0)

    def turn(u, cosine, sine):
        return u * cosine + pltpu.roll(u, LANES // 2, 1) * sine

    scale = 1.0 / math.sqrt(HEAD_DIM)
    mine = rows_at((c - 2 * m) * rows, rows)

    def attend(j):
        here = cols(j, LANES)
        q, k, v, grad = qkv[j, 0, mine], qkv[j, 1, mine], qkv[j, 2, mine], ogbuf[:, here]
        allowed = lax.broadcasted_iota(jnp.int32, (rows, rows), 0) >= lax.broadcasted_iota(
            jnp.int32, (rows, rows), 1
        )
        scores = jnp.where(allowed, dot_t(q, k) * scale, -jnp.inf)
        highest = jnp.max(scores, axis=-1, keepdims=True)
        expo = jnp.exp(scores - highest)
        probs = expo * (1.0 / jnp.sum(expo, axis=-1, keepdims=True))
        probs_b = probs.astype(bf16)
        out = jnp.dot(probs_b, v, preferred_element_type=f32).astype(bf16)
        osend[j] = out[hl:]

        @pl.when(h == 0)
        def _():
            out_ref[:, here] = out

        @pl.when(h == 1)
        def _():
            o_out(j).start()
            out_ref[pl.ds(hl, hl), here] = out[:hl]

        dprob = dot_t(grad, v)
        delta = jnp.sum(grad.astype(f32) * out.astype(f32), axis=-1, keepdims=True)
        dscore_b = (probs * (dprob - delta) * scale).astype(bf16)
        dq = jnp.dot(dscore_b, k, preferred_element_type=f32)
        dq = turn(dq, ctab[mine, :], -stab[mine, :]).astype(bf16)
        dv = t_dot(probs_b, grad).astype(bf16)
        lgacc[...] += 2.0 * (dot_t(ball[0, :, here], dq) + dot_t(ball[2, :, here], dv))
        low = lowt[c - 2 * m]
        gbs[j, 0:8, :] = (2.0 * jnp.dot(low, dq, preferred_element_type=f32))[0:8]
        gbs[j, 8:16, :] = (2.0 * jnp.dot(low, dv, preferred_element_type=f32))[8:16]
        for k_ in range(1, 4):
            gb_out(j, k_).start()

    def reach_two():
        pl.semaphore_wait(second_sem, beside)
        greet(third_sem)

    def reach_three():
        pl.semaphore_wait(third_sem, beside)
        for k in range(1, 4):
            pos_out(k).start()

    def factors_in():
        for copy in factors:
            copy.wait()
        nothing = jnp.zeros((8, 4 * LANES), f32)
        ball[0] = jnp.concatenate([bqbuf[...].astype(f32), nothing], axis=0).astype(bf16)
        ball[1] = jnp.concatenate([nothing, nothing], axis=0).astype(bf16)
        ball[2] = jnp.concatenate([nothing, bvbuf[...].astype(f32)], axis=0).astype(bf16)
        lgacc[...] = jnp.zeros(lgacc.shape, f32)

    def og_in():
        @pl.when(h == 1)
        def _():
            og_out.wait_recv()
            own_og[1].wait()

        @pl.when(h == 0)
        def _():
            own_og[0].wait()
            own_og[1].wait()

    @pl.when(inner)
    def _():
        e = jnp.where(home, 1, 0)

        @pl.when(home)
        def _():
            for half in range(2):
                for p in range(NP):
                    h_twin(c, half, p, own_piece(half, p)).start()

        @pl.when(away)
        def _():
            for p in range(NP):
                h_relay_in(p).start()
                h_direct(p).start()

        def z_in(b, p):
            h_arrived(b, e, p, s).wait_recv()
            h_cross(b, e, p).start()
            h_twin(b, e, p).start()

        def x_in(b, half, p):
            h_arrived(b, half, p, s).wait_recv()
            h_twin(b, half, p).start()

        def twin_in(b):
            for half in range(2):
                for p in range(NP):
                    h_arrived(b, half, p, 1 - s).wait_recv()

        def forward(j, t):
            for w in range(WP):
                copy = w_pass(j, t, w)
                copy.wait_recv()
                copy.start()

        def passed(j, t):
            for w in range(WP):
                w_arrived(j, t, w).wait_recv()

        def group_rows(g):
            return rows_at(g * rows, rows)

        def side_rows(side):
            return rows_at(side * 2 * rows, 2 * rows)

        def partner(j, t, g):
            here = half_of(g, 1 - m)
            group = jnp.where(g == 0, 3 - c, 3 * (1 - m))
            y = jnp.dot(hbuf[group_rows(group), :], wbuf[j, t], preferred_element_type=f32)
            psend[j, t, here] = y.astype(bf16)
            p_out(j, t, g).start()

        def partner_both(j, t):
            y = jnp.dot(hbuf[side_rows(1 - m), :], wbuf[j, t], preferred_element_type=f32)
            psend[j, t] = y.astype(bf16)
            p_out(j, t, 1).start()
            p_out(j, t, 0).start()

        whole = [(half, p) for half in range(2) for p in range(NP)]
        pieces = [(t, w) for t in range(3) for w in range(WP)]
        rest = list(pieces)

        def forward_piece(j, t, w):
            copy = w_pass(j, t, w)
            copy.wait_recv()
            copy.start()

        for p in range(NP):

            @pl.when(home)
            def _():
                h_relay_in(p).wait_recv()
                h_relay_out(p).start()

            if p == 0:
                reach_two()
            z_in(3 - c, p)
            if p == 0:
                reach_three()
            forward_piece(0, *rest.pop(0))

        @pl.when(home)
        def _():
            for half, p in whole[:2]:
                h_cross(c, half, p, own_piece(half, p)).start()

        while rest:
            forward_piece(0, *rest.pop(0))
        pl.when(h == 1)(og_out.start)
        far = 3 * (1 - m)
        late = (c == 1) & (h == 1)

        def first_in(t, carry):
            partner(0, t, 0)
            return carry

        def first_out(t, carry):
            partner(0, t, 1)
            return carry

        for p in range(NP // 2):
            z_in(far, p)
        for p in range(NP):
            x_in(3 - c, 1 - e, p)
            if p + NP // 2 < NP - 1:
                z_in(far, p + NP // 2)
        twin_in(3 - c)

        @pl.when(home)
        def _():
            for copy in own_h:
                copy.wait()
            twin_in(c)

        for t in range(3):
            own_w(0, t).wait()
            passed(0, t)

        @pl.when(jnp.logical_not(late))
        def _():
            lax.fori_loop(0, 3, first_in, 0)

        z_in(far, NP - 1)
        factors_in()
        tables()
        for p in range(NP):
            z_in(rim, p)
            x_in(far, 1 - e, p)

        @pl.when(home)
        def _():
            for half, p in whole[2:]:
                h_cross(c, half, p, own_piece(half, p)).start()

        twin_in(far)

        @pl.when(late)
        def _():
            lax.fori_loop(0, 3, first_in, 0)

        @pl.when(jnp.logical_not(late))
        def _():
            lax.fori_loop(0, 3, first_out, 0)

        forward(1, 0)
        for p in range(NP):
            x_in(rim, 1 - e, p)
        twin_in(rim)

        @pl.when(late)
        def _():
            lax.fori_loop(0, 3, first_out, 0)

        for j in range(1, 4):
            for t in range(3):
                own_w(j, t).wait()
        a_both = jnp.concatenate(
            [
                aqbuf[:, pl.ds(pl.multiple_of(m * 2 * width, LANES), 2 * width)].astype(f32),
                avbuf[:, pl.ds(pl.multiple_of(m * 2 * width, LANES), 2 * width)].astype(f32),
            ],
            axis=0,
        ).astype(bf16)

        def low_other(g, carry):
            group = 2 * (1 - m) + g
            lsend[g] = dot_t(a_both, hbuf[group_rows(group), :])
            l_out(g).start()
            return carry

        forward(1, 1)
        lax.fori_loop(0, 2, low_other, 0)

        def low_own(g, carry):
            group = 2 * m + g
            l_out(g).wait_recv()
            lowt[g] = (dot_t(a_both, hbuf[group_rows(group), :]) + lrecv[g]).astype(bf16)
            return carry

        def finish(i):
            j, t = i // 3, lax.rem(i, 3)
            plain = t == 2

            low = jnp.concatenate([lowt[0], lowt[1]], axis=1)
            y = jnp.dot(hbuf[side_rows(m), :], wbuf[j, t], preferred_element_type=f32)
            y = y + 2.0 * t_dot(low, ball[t, :, cols(j, LANES)])
            held[...] = y
            for g in (1, 0):
                here = half_of(g, m)
                cosine = jnp.where(plain, 1.0, ctab[here, :])
                sine = jnp.where(plain, 0.0, stab[here, :])
                p_out(j, t, g, m).wait_recv()
                whole_y = held[here, :] + precv[j, t, here].astype(f32)
                qkv[j, t, here] = turn(whole_y, cosine, sine).astype(bf16)
                if g == 1:
                    q_out(j, t).start()

        def slot(i, carry):
            @pl.when(i < 13)
            def _():
                j, t = (i - 1) // 3, lax.rem(i - 1, 3)
                passed(j, t)

                partner_both(j, t)

            @pl.when(i < 11)
            def _():
                forward((i + 1) // 3, lax.rem(i + 1, 3))

            @pl.when(i == 6)
            def _():
                @pl.when(away)
                def _():
                    for half, p in whole:
                        x_in(c, half, p)
                    twin_in(c)

                lax.fori_loop(0, 2, low_own, 0)
                lq_out.start()

            first = jnp.where(i == 6, 0, jnp.where(i == 7, 2, i - 4))
            count = jnp.where(i < 6, 0, jnp.where(i < 8, 2, 1))

            def some(k, carry_):
                finish(first + k)
                return carry_

            lax.fori_loop(0, count, some, 0)

            pl.when(i == 7)(og_in)

            @pl.when((i == 7) | (i == 9) | (i == 12) | (i == 15))
            def _():
                attend(jnp.where(i == 15, 3, (i - 6) // 2 - jnp.where(i == 12, 1, 0)))

            return carry

        lax.fori_loop(4, 16, slot, 0)

    @pl.when(outer)
    def _():
        for t in range(3):
            for w in range(WP):
                w_out(0, t, w).start()
        for p in range(NP):
            h_relay_in(p).start()
        reach_two()
        reach_three()

        def relays():
            for p in range(NP):
                h_relay_in(p).wait_recv()
                h_relay_out(p).start()

        @pl.when(home)
        def _():
            relays()
            for p in range(NP):
                h_direct(p).start()

        @pl.when(away)
        def _():
            for p in range(NP):
                h_direct(p).start()
            relays()

        def send_w(j, carry):
            for t in range(3):
                for w in range(WP):
                    remote(
                        weights[t].at[rows_at(r * (depth // 2) + w * wrows, wrows), cols(j, LANES)],
                        wslot(j, t, c - 2 * m, r, w),
                        w_send.at[j, t, w],
                        w_recv.at[j, t, r, w],
                        {"ctx": near},
                    ).start()
            return carry

        send_w(1, 0)
        pl.when(h == 1)(og_out.start)
        lax.fori_loop(2, 4, send_w, 0)
        factors_in()
        tables()
        og_in()
        remote(lowt.at[m], lowt.at[m], lq_send.at[0], lq_recv.at[0], {"sub": 1 - s}).wait_recv()

        def one(j, carry):
            for t in range(3):
                q_out(j, t).wait_recv()
            attend(j)
            return carry

        lax.fori_loop(0, 4, one, 0)

    lgs[...] = lgacc[...].astype(bf16)
    lgr[me] = lgs[...]

    def lg_out(k):
        dest = 4 + k
        return remote(lgs, lgr.at[me], lg_send.at[k], lg_recv.at[me], member(dest))

    for k in range(8):
        pl.when(me != 4 + k)(lg_out(k).start)

    for p in range(NP):
        pl.when(direct_on)(h_direct(p).wait_send)
        pl.when(direct_on)(h_relay_in(p).wait_send)
        pl.when(relay_on)(h_relay_out(p).wait_send)
    for k in range(1, 4):
        pos_out(k).wait_send()
    pl.when(h == 1)(og_out.wait_send)

    @pl.when(outer)
    def _():
        for j in range(4):
            for t in range(3):
                for w in range(WP):
                    w_out(j, t, w).wait_send()

    @pl.when(inner)
    def _():
        for b in range(4):
            for half in range(2):
                for p in range(NP):
                    h_twin(b, half, p).wait_send()
                    crossed = ((b == c) & home) | ((b != c) & (home == (half == 1)))
                    pl.when(crossed)(h_cross(b, half, p).wait_send)
        for j in range(4):
            for t in range(3):
                for w in range(WP):
                    w_pass(j, t, w).wait_send()
                for g in range(2):
                    p_out(j, t, g).wait_send()
                q_out(j, t).wait_send()
        for g in range(2):
            l_out(g).wait_send()
        lq_out.wait_send()

    def ga_out(k):
        dest = lax.rem(me + k, 16)
        return remote(gas, gar.at[me - 4], ga_send.at[k - 1], ga_recv.at[me - 4], member(dest))

    @pl.when(inner)
    def _():
        for k in range(1, 16):
            frm = lax.rem(me + k, 16)
            remote(lgs, lgr.at[frm], lg_send.at[0], lg_recv.at[frm], {"sub": 1 - s}).wait_recv()

        def side(hd):
            return jnp.concatenate(
                [
                    lgr[4 * g + 2 * hd].astype(f32) + lgr[4 * g + 2 * hd + 1].astype(f32)
                    for g in range(4)
                ],
                axis=1,
            )

        zero, one = side(0), side(1)
        wide_ = 4 * rows
        right = jnp.concatenate([one[:, wide_ - hl :], one[:, : wide_ - hl]], axis=1)
        left = jnp.concatenate([zero[:, hl:], zero[:, :hl]], axis=1)
        low = jnp.where(h == 0, zero + right, left + one)
        upper = low.astype(bf16)
        lower = (low - upper.astype(f32)).astype(bf16)
        both = jnp.concatenate([upper, lower], axis=0)
        part_ = jnp.dot(both, hbuf[:, cols(h * 2 + s, slice_k)], preferred_element_type=f32)
        gas[...] = (part_[0:16] + part_[16:32]).astype(bf16)
        gar[me - 4] = gas[...]
        for k in range(1, 16):
            ga_out(k).start()

    @pl.when(h == 1)
    def _():
        for j in range(4):
            o_out(j).wait_recv()
            out_ref[0:hl, j * LANES : (j + 1) * LANES] = orecv[j]

    for j in range(4):
        for block in range(4):

            @pl.when(block != c)
            def _():
                remote(gbs.at[0], gbr.at[block, j], gb_send.at[0, 0], gb_recv.at[j, block], {"sub": 1 - s}).wait_recv()

        gbr[c, j] = gbs[j]
        total = (gbr[0, j] + gbr[1, j]) + (gbr[2, j] + gbr[3, j])
        gbq_ref[:, j * LANES : (j + 1) * LANES] = total[0:8]
        gbv_ref[:, j * LANES : (j + 1) * LANES] = total[8:16]

    for k in range(8):

        @pl.when(me != 4 + k)
        def _():
            remote(gas, gar.at[k], ga_send.at[0], ga_recv.at[k], {"sub": 1 - s}).wait_recv()

        block = gar[k].astype(f32)
        gaq_ref[:, k * slice_k : (k + 1) * slice_k] = block[0:8]
        gav_ref[:, k * slice_k : (k + 1) * slice_k] = block[8:16]

    @pl.when(h == 1)
    def _():
        for j in range(4):
            o_out(j).wait_send()

    for j in range(4):
        for k in range(1, 4):
            gb_out(j, k).wait_send()
    for k in range(8):
        pl.when(me != 4 + k)(lg_out(k).wait_send)

    @pl.when(inner)
    def _():
        for k in range(1, 16):
            ga_out(k).wait_send()


def hand_over_kernel(count, *refs):
    sources, results, stages, sems = refs[:count], refs[count : 2 * count], refs[2 * count : 3 * count], refs[-1]
    fetched = [pltpu.make_async_copy(sources[k], stages[k], sems.at[0, k]) for k in range(count)]
    stored = [pltpu.make_async_copy(stages[k], results[k], sems.at[1, k]) for k in range(count)]
    for copy in fetched:
        copy.start()
    for k in reversed(range(count)):
        fetched[k].wait()
        stored[k].start()
    for copy in stored:
        copy.wait()


def hand_over(*arrays):
    spec = pl.BlockSpec(memory_space=pl.ANY)
    count = len(arrays)
    return pl.pallas_call(
        functools.partial(hand_over_kernel, count),
        out_shape=tuple(jax.ShapeDtypeStruct(a.shape, a.dtype) for a in arrays),
        in_specs=[spec] * count,
        out_specs=[spec] * count,
        scratch_shapes=[pltpu.VMEM(a.shape, a.dtype) for a in arrays] + [pltpu.SemaphoreType.DMA((2, count))],
    )(*arrays)


def paired(
    hidden_states, w_query, w_key, w_value, a_query, a_value, b_query, b_value, positions, out_grad
):
    f32, bf16 = jnp.float32, jnp.bfloat16
    rows, width = hidden_states.shape
    model, rank = a_query.shape
    depth, columns = w_query.shape
    pos = positions.reshape(rows // LANES, LANES)
    vmem, dma = pltpu.VMEM, pltpu.SemaphoreType.DMA
    hbm_spec = pl.BlockSpec(memory_space=pl.ANY)
    vmem_spec = pl.BlockSpec(memory_space=pltpu.VMEM)
    out, gaq, gbq, gav, gbv = pl.pallas_call(
        paired_kernel,
        out_shape=(
            jax.ShapeDtypeStruct((rows, columns), bf16),
            jax.ShapeDtypeStruct((rank, model), f32),
            jax.ShapeDtypeStruct((rank, columns), f32),
            jax.ShapeDtypeStruct((rank, model), f32),
            jax.ShapeDtypeStruct((rank, columns), f32),
        ),
        in_specs=[hbm_spec] * 10,
        out_specs=[vmem_spec] * 5,
        scratch_shapes=[
            vmem((4 * rows, 2 * width), bf16),
            vmem((4, 3, 2 * depth, LANES), bf16),
            vmem((rows // 2, width), bf16),
            vmem((4, 3, 2 * rows, LANES), bf16),
            vmem((4, 3, 2 * rows, LANES), bf16),
            vmem((2, 16, rows), f32),
            vmem((2, 16, rows), f32),
            vmem((4, 3, 2 * rows, LANES), bf16),
            vmem((2 * rows, LANES), f32),
            vmem((2, 16, rows), bf16),
            vmem((3, 16, columns), bf16),
            vmem((rows, columns), bf16),
            vmem((4, rows // LANES, LANES), jnp.int32),
            vmem((2 * rows, LANES), f32),
            vmem((2 * rows, LANES), f32),
            vmem((4, rows // 2, LANES), bf16),
            vmem((4, rows // 2, LANES), bf16),
            vmem((4, 16, LANES), f32),
            vmem((4, 4, 16, LANES), f32),
            vmem((16, rows), f32),
            vmem((16, rows), bf16),
            vmem((16, 16, rows), bf16),
            vmem((16, model // 8), bf16),
            vmem((8, 16, model // 8), bf16),
            vmem((rank, model), bf16),
            vmem((rank, model), bf16),
            vmem((rank, columns), bf16),
            vmem((rank, columns), bf16),
            pltpu.SemaphoreType.REGULAR,
            pltpu.SemaphoreType.REGULAR,
            dma((21,)),
            dma((2, NP)),
            dma((NP,)),
            dma((NP,)),
            dma((4, 2, NP)),
            dma((4, 2, NP)),
            dma((4, 2, NP, 2)),
            dma((4, 3, WP)),
            dma((4, 3, WP)),
            dma((4, 3, 2, WP)),
            dma((4, 3, 2)),
            dma((4, 3, 2)),
            dma((2,)),
            dma((2,)),
            dma((4, 3)),
            dma((4, 3)),
            dma((1,)),
            dma((1,)),
            dma((1,)),
            dma((1,)),
            dma((3,)),
            dma((4,)),
            dma((4,)),
            dma((4,)),
            dma((4, 3)),
            dma((4, 4)),
            dma((8,)),
            dma((16,)),
            dma((15,)),
            dma((8,)),
        ],
        compiler_params=pltpu.CompilerParams(
            collective_id=1, has_side_effects=True, vmem_limit_bytes=56 * 1024 * 1024
        ),
    )(
        hidden_states, w_query, w_key, w_value, a_query.T, a_value.T, b_query, b_value, pos, out_grad
    )
    out, gaq, gbq, gav, gbv = hand_over(out, gaq, gbq, gav, gbv)
    return (out, gaq.T, gbq, gav.T, gbv)


def fits_paired(mesh, args):
    hidden_states, w_query, a_query = args[0], args[1], args[4]
    return (
        mesh.shape["rep"] == 2
        and mesh.shape["ctx"] == 4
        and mesh.shape["head"] == 2
        and mesh.shape["sub"] == 2
        and w_query.shape[1] == 4 * HEAD_DIM
        and HEAD_DIM == LANES
        and HEADS == 16
        and a_query.shape[1] == 8
        and hidden_states.shape[0] == 2 * LANES
        and hidden_states.shape[1] == w_query.shape[0]
        and a_query.shape[0] == 4 * w_query.shape[0]
        and w_query.shape[0] == 1024
    )


def choose(mesh, *args):
    return paired(*args) if fits_paired(mesh, args) else local(*args)


def solution(mesh):
    in_specs = (
        P(("rep", "ctx"), ("head", "sub")),
        P("ctx", ("head", "sub")),
        P("ctx", ("head", "sub")),
        P("ctx", ("head", "sub")),
        P(),
        P(),
        P(None, ("head", "sub")),
        P(None, ("head", "sub")),
        P(("rep", "ctx")),
        P(("rep", "ctx"), ("head", "sub")),
    )
    out_specs = (
        P(("rep", "ctx"), ("head", "sub")),
        P(None, "rep"),
        P("rep", ("head", "sub")),
        P(None, "rep"),
        P("rep", ("head", "sub")),
    )
    return jax.shard_map(
        functools.partial(choose, mesh), mesh=mesh, in_specs=in_specs, out_specs=out_specs, check_vma=False
    )
```
